1024 devices in a mesh: aa: 32 (over x, z_lo), col: 4 (over z_hi, core), pb: 8 (over y).
Axes of the slice: x: 8, y: 8, z: 8 (z_hi: 2, z_lo: 4; z = z_hi * 4 + z_lo), core: 2. Of those that a mesh axis runs over, the one named last changes fastest.
Arguments:
- b_ac: bfloat16 [1536, 512, 1024], P('pb', 'aa', 'col'), may hold values from -6 to 6
- b_oc: bfloat16 [1536, 32, 1024], P('pb', None, 'col'), may hold values from -6 to 6
- t1: bfloat16 [32, 512], P(None, 'aa'), may hold values from -0.59765625 to 0.59765625
- f_bd: bfloat16 [1536, 256], P('pb'), may hold values from -0.15625 to 0.15625
- t2: bfloat16 [512, 32768], P('aa', ('col', 'pb')), may hold values from -0.0625 to 0.0625
Outputs:
- residual: float32 [512, 4096], P(('col', 'pb'), 'aa')
The draws below stay inside these ranges and needn't reach their ends.
All inputs are finite; a program needn't handle non-finite values.
Results may differ from the reference program's by a relative error of at most 0.0041.
Values may be sent and summed in bfloat16 or wider, within the bound.
No kernel may reach another device: no remote copies, remote signals or barrier semaphores. Data moves between devices by JAX's collectives and lax.ppermute only.
A program may use at most 32 MiB of HBM per device.

```python
import jax
import jax.numpy as jnp
from jax import lax

V = 1024
VA = 512
NAUX = 1536
NOCC = 32
BB = 8
DB = 32
PAIRS = 512
N_AA = 32


def raised(result, key, source, target, shards_of, factor):
    def block_of(axis_at):
        return (jnp.arange(result.shape[axis_at]) // (result.shape[axis_at] // shards_of)).reshape((-1,) + (1,) * (result.ndim - 1 - axis_at))

    near = jax.random.permutation(key, shards_of)[block_of(target)]
    second = (block_of(target) + shards_of // 2) % shards_of
    return jnp.where((block_of(source) == near) | (block_of(source) == second), factor * result, result)


def levels(key, dims, cuts, smallest, high):
    gain = 1.0
    for dim, blocks in cuts:
        draws = jax.random.uniform(jax.random.fold_in(jax.random.fold_in(key, 6), dim), (blocks,), jnp.float32, smallest / len(cuts), high / len(cuts))
        gain = gain * jnp.repeat(jnp.exp(draws), dims[dim] // blocks).reshape((-1,) + (1,) * (len(dims) - 1 - dim))
    return gain


def noise(rng, dims, scale, reach, pieces=(), kind=jnp.bfloat16):
    drawn = scale * jax.random.normal(rng, dims, jnp.float32)
    if pieces:
        drawn = drawn * levels(rng, dims, pieces, -0.22, 0.18)
    return jnp.clip(drawn, -reach, reach).astype(kind)


def gaussian_with(rng, extent, deviation, bound, cuts, heavy, kind=jnp.bfloat16):
    drawn = deviation * jax.random.normal(rng, extent, jnp.float32)
    if cuts:
        drawn = drawn * levels(rng, extent, cuts, -0.22, 0.18)
    return jnp.clip(raised(drawn, jax.random.fold_in(rng, 3), *heavy), -bound, bound).astype(kind)


def setup_inputs(seed: int = 0) -> dict:
    splits = jax.random.split(jax.random.key(seed), 6)
    return {
        "b_ac": noise(splits[0], (NAUX, VA, V), 1.0, 6.0, ((0, 8), (1, 32), (2, 4))),
        "b_oc": noise(splits[1], (NAUX, NOCC, V), 1.0, 6.0, ((0, 8), (2, 4))),
        "t1": noise(splits[2], (NOCC, VA), 0.1, 0.59765625, ((1, 32),)),
        "f_bd": noise(splits[3], (NAUX, BB * DB), NAUX ** -0.5, 0.15625, ((0, 8),)),
        "t2": gaussian_with(splits[4], (PAIRS, V * DB), (V * DB) ** -0.5, 0.0625, ((0, 32), (1, 32)), (1, 0, 32, 2.75)),
    }


def reference(b_ac, b_oc, t1, f_bd, t2):
    width = VA // N_AA
    b_occ = b_oc.astype(jnp.float32)

    def one_block(index):
        offset = (index * width).astype(jnp.int32)
        slab = lax.dynamic_slice_in_dim(b_ac, offset, width, 1).astype(jnp.float32)
        singles = lax.dynamic_slice_in_dim(t1, offset, width, 1).astype(jnp.float32)
        correction = jnp.einsum('ka,qkc->qac', singles, b_occ)
        dressed = (slab - correction).astype(jnp.bfloat16)
        ladder = lax.dot_general(dressed.reshape(NAUX, width * V), f_bd, (((0,), (0,)), ((), ())), preferred_element_type=jnp.float32).astype(jnp.bfloat16)
        ladder = ladder.reshape(width, V, BB, DB).transpose(0, 2, 1, 3).reshape(width * BB, V * DB)
        return lax.dot_general(t2, ladder, (((1,), (1,)), ((), ())), preferred_element_type=jnp.float32)

    blocks = lax.map(one_block, jnp.arange(N_AA, dtype=jnp.int32))
    return blocks.transpose(1, 0, 2).reshape(PAIRS, VA * BB)
```

```python
import jax
import jax.numpy as jnp
from jax import lax
from jax.experimental import pallas as pl
from jax.experimental.pallas import tpu as pltpu
from jax.sharding import PartitionSpec as P


BB = 8
DB = 32
Z_RUN = 4
LANES = 128
LANE_GROUPS = LANES // DB


def from_aa(array, x_step, z_flip):
    n_x = lax.axis_size("aa") // Z_RUN
    pairs = [
        (x * Z_RUN + z, (x + x_step) % n_x * Z_RUN + (z ^ z_flip))
        for x in range(n_x)
        for z in range(Z_RUN)
    ]
    return lax.ppermute(array, "aa", pairs)


def gather_amplitudes(t2):
    n_x = lax.axis_size("aa") // Z_RUN
    near = [t2] + [from_aa(t2, 0, flip) for flip in range(1, Z_RUN)]
    near = jnp.stack(near)
    far = [near] + [from_aa(near, step, 0) for step in range(1, n_x)]
    return far


def combine_kernel(place_ref, pieces_ref, *refs):
    far_refs, (out_ref, ladder_ref, turned_ref, factor_ref, t2_ref) = refs[:-5], refs[-5:]
    n_far = len(far_refs)
    rows = far_refs[0].shape[1]
    for step_back, far_ref in enumerate(far_refs):
        for flip in range(Z_RUN):
            at = (step_back * Z_RUN + flip) * rows
            t2_ref[at : at + rows, :] = far_ref[flip]
    total = pieces_ref[0].astype(jnp.float32)
    for shard in range(1, pieces_ref.shape[0]):
        total += pieces_ref[shard].astype(jnp.float32)
    for b_high in range(BB // LANE_GROUPS):
        ladder_ref[b_high] = total[:, b_high * LANES : (b_high + 1) * LANES]
    n_rows = total.shape[0] // LANE_GROUPS
    group = lax.broadcasted_iota(jnp.int32, (n_rows, LANES), 1) // DB

    def pick(by_group):
        chosen = by_group[0]
        for lane_group in range(1, LANE_GROUPS):
            chosen = jnp.where(group == lane_group, by_group[lane_group], chosen)
        return chosen

    for b_high in range(BB // LANE_GROUPS):
        by_c = [
            ladder_ref.at[b_high][pl.ds(c_low, n_rows, stride=LANE_GROUPS), :]
            for c_low in range(LANE_GROUPS)
        ]
        skewed = []
        for turn in range(LANE_GROUPS):
            mixed = pick([by_c[(b_low + turn) % LANE_GROUPS] for b_low in range(LANE_GROUPS)])
            skewed.append(pltpu.roll(mixed, turn * DB, 1) if turn else mixed)
        for b_low in range(LANE_GROUPS):
            b = b_high * LANE_GROUPS + b_low
            by_b = pick([skewed[(c_low - b_low) % LANE_GROUPS] for c_low in range(LANE_GROUPS)])
            for a in range(n_rows // BB):
                at = (a * BB + b) * BB
                turned_ref[at : at + BB, :] = by_b[a * BB : (a + 1) * BB]
    for c_high in range(BB):
        tile = turned_ref[pl.ds(c_high, n_rows, stride=BB), :]
        factor_ref[:, c_high * LANES : (c_high + 1) * LANES] = tile.astype(jnp.bfloat16)
    sums = lax.dot_general(
        t2_ref[...],
        factor_ref[...],
        (((1,), (1,)), ((), ())),
        preferred_element_type=jnp.float32,
    )
    x, z = place_ref[0] // Z_RUN, place_ref[0] % Z_RUN
    for step_back in range(n_far):
        source_x = lax.rem(x + (n_far - step_back), n_far)
        for flip in range(Z_RUN):
            at = (step_back * Z_RUN + flip) * rows
            out_ref[source_x * Z_RUN + (z ^ flip)] = sums[at : at + rows]


def combine(pieces, far, a_width, c_block):
    rows, cd_width = far[0].shape[1:]
    n_aa = len(far) * Z_RUN
    ab_width = a_width * BB
    whole = pl.BlockSpec(memory_space=pltpu.VMEM)
    return pl.pallas_call(
        combine_kernel,
        out_shape=jax.ShapeDtypeStruct((n_aa, rows, ab_width), jnp.float32),
        in_specs=[pl.BlockSpec(memory_space=pltpu.SMEM)] + [whole] * (1 + len(far)),
        out_specs=whole,
        scratch_shapes=[
            pltpu.VMEM((BB // LANE_GROUPS, a_width * c_block, LANES), jnp.float32),
            pltpu.VMEM((ab_width * BB, LANES), jnp.float32),
            pltpu.VMEM((ab_width, cd_width), jnp.bfloat16),
            pltpu.VMEM((n_aa * rows, cd_width), jnp.bfloat16),
        ],
        cost_estimate=pl.CostEstimate(
            flops=2 * n_aa * rows * ab_width * cd_width, bytes_accessed=3 << 20, transcendentals=0
        ),
    )(lax.axis_index("aa").astype(jnp.int32).reshape(1), pieces, *far)


def step(b_ac, b_oc, t1, f_bd, t2):
    n_pb = lax.axis_size("pb")
    _, a_width, c_width = b_ac.shape
    c_block = c_width // n_pb

    far = gather_amplitudes(t2)

    correction = jnp.einsum("ka,qkc->qac", t1, b_oc, preferred_element_type=jnp.float32)
    dressed = (b_ac - correction).astype(jnp.bfloat16)
    partial = jnp.einsum("qac,qn->acn", dressed, f_bd, preferred_element_type=jnp.float32)
    partial = (
        partial.astype(jnp.bfloat16)
        .reshape(a_width, n_pb, c_block, BB * DB)
        .transpose(1, 0, 2, 3)
        .reshape(n_pb, a_width * c_block, BB * DB)
    )
    pieces = lax.all_to_all(partial, "pb", 0, 0, tiled=True)
    pieces, *far = lax.optimization_barrier((pieces, *far))
    sums = combine(pieces, far, a_width, c_block)
    shares = lax.all_to_all(sums, ("col", "pb"), 0, 0, tiled=True)
    return jnp.sum(shares, axis=0)


def solution(mesh):
    placed = (
        P("pb", "aa", "col"),
        P("pb", None, "col"),
        P(None, "aa"),
        P("pb", None),
        P("aa", ("col", "pb")),
    )
    return jax.shard_map(
        step, mesh=mesh, in_specs=placed, out_specs=P(("col", "pb"), "aa"), check_vma=False
    )
```

```python
import jax
import jax.numpy as jnp
from jax import lax
from jax.experimental import pallas as pl
from jax.experimental.pallas import tpu as pltpu
from jax.sharding import PartitionSpec as P


BB = 8
DB = 32
LANES = 128
LANE_GROUPS = LANES // DB
VMEM = pl.BlockSpec(memory_space=pltpu.VMEM)
SMEM = pl.BlockSpec(memory_space=pltpu.SMEM)


def split_kernel(place_ref, ladder_ref, up_ref, down_ref, across_ref, up2_ref, down2_ref, own_ref):
    a_width, c_width, _ = ladder_ref.shape
    c_block = own_ref.shape[0] // a_width
    n_pb = c_width // c_block
    for distance, out_ref in (
        (1, up_ref.at[0]),
        (3, up_ref.at[1]),
        (n_pb - 1, down_ref.at[0]),
        (n_pb - 3, down_ref.at[1]),
        (4, across_ref),
        (2, up2_ref),
        (n_pb - 2, down2_ref),
        (0, own_ref),
    ):
        c_at = pl.multiple_of(lax.rem(place_ref[0] + distance, n_pb) * c_block, c_block)
        for a in range(a_width):
            out_ref[a * c_block : (a + 1) * c_block, :] = ladder_ref[a, pl.ds(c_at, c_block), :]


def split(ladder, place, n_pb):
    a_width, c_width, bd_width = ladder.shape
    block = (a_width * c_width // n_pb, bd_width)
    shapes = [(2, *block)] * 2 + [block] * 4
    return pl.pallas_call(
        split_kernel,
        out_shape=[jax.ShapeDtypeStruct(shape, ladder.dtype) for shape in shapes],
        in_specs=[SMEM, VMEM],
        out_specs=[VMEM] * 6,
        cost_estimate=pl.CostEstimate(flops=0, bytes_accessed=4 << 20, transcendentals=0),
    )(place, ladder)


def merge_kernel(core_ref, up_ref, down_ref, across_ref, up2_ref, down2_ref, up_out, down_out):
    across = across_ref[...].astype(jnp.float32)
    zero = jnp.zeros_like(across)
    for core, passing_ref, own_ref, out_ref in (
        (0, up_ref, up2_ref, up_out),
        (1, down_ref, down2_ref, down_out),
    ):
        total = own_ref[...].astype(jnp.float32) + passing_ref[1].astype(jnp.float32)
        total += jnp.where(core_ref[0] == core, across, zero)
        out_ref[...] = total.astype(out_ref.dtype)


def merge(core, up, down, across, up2, down2):
    return pl.pallas_call(
        merge_kernel,
        out_shape=[jax.ShapeDtypeStruct(up2.shape, up2.dtype)] * 2,
        in_specs=[SMEM] + [VMEM] * 5,
        out_specs=[VMEM] * 2,
        cost_estimate=pl.CostEstimate(flops=4 * up2.size, bytes_accessed=2 << 20, transcendentals=0),
    )(core, up, down, across, up2, down2)


def combine_kernel(
    own_ref, up_ref, down_ref, up2_ref, down2_ref, t2_ref, out_ref, ladder_ref, turned_ref, factor_ref
):
    total = own_ref[...].astype(jnp.float32)
    total += up_ref[0].astype(jnp.float32)
    total += down_ref[0].astype(jnp.float32)
    total += up2_ref[...].astype(jnp.float32)
    total += down2_ref[...].astype(jnp.float32)
    for b_high in range(BB // LANE_GROUPS):
        ladder_ref[b_high] = total[:, b_high * LANES : (b_high + 1) * LANES]
    n_rows = total.shape[0] // LANE_GROUPS
    group = lax.broadcasted_iota(jnp.int32, (n_rows, LANES), 1) // DB

    def pick(by_group):
        chosen = by_group[0]
        for lane_group in range(1, LANE_GROUPS):
            chosen = jnp.where(group == lane_group, by_group[lane_group], chosen)
        return chosen

    for b_high in range(BB // LANE_GROUPS):
        by_c = [
            ladder_ref.at[b_high][pl.ds(c_low, n_rows, stride=LANE_GROUPS), :]
            for c_low in range(LANE_GROUPS)
        ]
        skewed = []
        for turn in range(LANE_GROUPS):
            mixed = pick([by_c[(b_low + turn) % LANE_GROUPS] for b_low in range(LANE_GROUPS)])
            skewed.append(pltpu.roll(mixed, turn * DB, 1) if turn else mixed)
        for b_low in range(LANE_GROUPS):
            b = b_high * LANE_GROUPS + b_low
            by_b = pick([skewed[(c_low - b_low) % LANE_GROUPS] for c_low in range(LANE_GROUPS)])
            for a in range(n_rows // BB):
                at = (a * BB + b) * BB
                turned_ref[at : at + BB, :] = by_b[a * BB : (a + 1) * BB]
    for c_high in range(BB):
        tile = turned_ref[pl.ds(c_high, n_rows, stride=BB), :]
        factor_ref[:, c_high * LANES : (c_high + 1) * LANES] = tile.astype(jnp.bfloat16)
    out_ref[...] = lax.dot_general(
        t2_ref[...],
        factor_ref[...],
        (((1,), (1,)), ((), ())),
        preferred_element_type=jnp.float32,
    )


def combine(parts, t2):
    block_rows, bd_width = parts[0].shape
    pairs, cd_width = t2.shape
    ab_width = block_rows * bd_width // cd_width
    return pl.pallas_call(
        combine_kernel,
        out_shape=jax.ShapeDtypeStruct((pairs, ab_width), jnp.float32),
        in_specs=[VMEM] * 6,
        out_specs=VMEM,
        scratch_shapes=[
            pltpu.VMEM((BB // LANE_GROUPS, block_rows, LANES), jnp.float32),
            pltpu.VMEM((ab_width * BB, LANES), jnp.float32),
            pltpu.VMEM((ab_width, cd_width), jnp.bfloat16),
        ],
        cost_estimate=pl.CostEstimate(
            flops=2 * pairs * ab_width * cd_width, bytes_accessed=3 << 20, transcendentals=0
        ),
    )(*parts, t2)


def along_pb(array, distance):
    n_pb = lax.axis_size("pb")
    return lax.ppermute(array, "pb", [(y, (y + distance) % n_pb) for y in range(n_pb)])


def across_pb(array, distance):
    n_pb = lax.axis_size("pb")
    pairs = []
    for col in range(lax.axis_size("col")):
        way = -distance if col % 2 else distance
        pairs += [(col * n_pb + y, col * n_pb + (y + way) % n_pb) for y in range(n_pb)]
    return lax.ppermute(array, ("col", "pb"), pairs)


def step(b_ac, b_oc, t1, f_bd, t2):
    n_aa = lax.axis_size("aa")
    n_pb = lax.axis_size("pb")
    n_out = lax.axis_size("col") * n_pb
    place = lax.axis_index("pb").astype(jnp.int32).reshape(1)
    core = lax.rem(lax.axis_index("col"), 2).astype(jnp.int32).reshape(1)

    amplitudes = lax.all_to_all(
        jnp.broadcast_to(t2[None], (n_aa, *t2.shape)), "aa", 0, 0, tiled=True
    ).reshape(-1, t2.shape[1])

    correction = jnp.einsum("ka,qkc->qac", t1, b_oc, preferred_element_type=jnp.float32)
    dressed = (b_ac - correction).astype(jnp.bfloat16)
    ladder = jnp.einsum(
        "qac,qn->acn", dressed, f_bd, preferred_element_type=jnp.float32
    ).astype(jnp.bfloat16)
    up, down, across, up2, down2, own = split(ladder, place, n_pb)
    up = along_pb(up, 1)
    down = along_pb(down, -1)
    across = across_pb(across, 2)
    up2, down2 = merge(core, up, down, across, up2, down2)
    up2 = along_pb(up2, 2)
    down2 = along_pb(down2, -2)
    *parts, amplitudes = lax.optimization_barrier((own, up, down, up2, down2, amplitudes))
    sums = combine(parts, amplitudes)
    shares = sums.reshape(n_out, -1, sums.shape[1])
    shares = lax.all_to_all(shares, ("col", "pb"), 0, 0, tiled=True)
    return jnp.sum(shares, axis=0)


def solution(mesh):
    placed = (
        P("pb", "aa", "col"),
        P("pb", None, "col"),
        P(None, "aa"),
        P("pb", None),
        P("aa", ("col", "pb")),
    )
    return jax.shard_map(
        step, mesh=mesh, in_specs=placed, out_specs=P(("col", "pb"), "aa"), check_vma=False
    )
```

```python
import jax
import jax.numpy as jnp
from jax import lax
from jax.experimental import pallas as pl
from jax.experimental.pallas import tpu as pltpu
from jax.sharding import PartitionSpec as P


BB = 8
DB = 32
LANES = 128
LANE_GROUPS = LANES // DB
Q_GROUP = 8
Q_STEPS = 4
VMEM = pl.BlockSpec(memory_space=pltpu.VMEM)
SMEM = pl.BlockSpec(memory_space=pltpu.SMEM)


def contract_kernel(place_ref, b_ac_ref, b_oc_ref, singles_ref, f_ref, *refs):
    out_refs, (dressed_ref, ladder_ref, sems) = refs[:-3], refs[-3:]
    n_q, a_width, c_width = b_ac_ref.shape
    n_total = dressed_ref.shape[1] // a_width
    n_pb, block_rows, _ = ladder_ref.shape
    c_block = block_rows // a_width
    size = Q_GROUP * a_width
    step = pl.program_id(0)
    for group in range(n_q // Q_GROUP):
        rows = slice(group * Q_GROUP, (group + 1) * Q_GROUP)
        occupied = b_oc_ref[rows].reshape(-1, c_width)
        correction = jnp.dot(singles_ref[...], occupied, preferred_element_type=jnp.float32)
        block = b_ac_ref[rows].reshape(size, c_width).astype(jnp.float32)
        dressed = (block - correction).astype(jnp.bfloat16).astype(jnp.float32)
        at = pl.ds(pl.multiple_of((step * (n_q // Q_GROUP) + group) * size, size), size)
        for half in range(c_width // LANES):
            dressed_ref[half, at, :] = dressed[:, half * LANES : (half + 1) * LANES]

    @pl.when(step == pl.num_programs(0) - 1)
    def _():
        factors = f_ref[...]
        for half in range(c_width // LANES):
            for a in range(a_width):
                slab = dressed_ref.at[half][pl.ds(a, n_total, stride=a_width), :]
                part = lax.dot_general(
                    slab.astype(jnp.bfloat16),
                    factors,
                    (((0,), (0,)), ((), ())),
                    preferred_element_type=jnp.float32,
                ).astype(ladder_ref.dtype)
                for c_at in range(0, LANES, c_block):
                    ladder_ref[(half * LANES + c_at) // c_block, a * c_block : (a + 1) * c_block, :] = (
                        part[c_at : c_at + c_block]
                    )
        copies = [
            pltpu.make_async_copy(
                ladder_ref.at[lax.rem(place_ref[0] + distance, n_pb)], out_ref, sems.at[distance]
            )
            for distance, out_ref in enumerate(out_refs)
        ]
        for copy in copies:
            copy.start()
        for copy in copies:
            copy.wait()


def contract(b_ac, b_oc, t1, f_bd, place, n_pb):
    n_q, a_width, c_width = b_ac.shape
    n_occ = b_oc.shape[1]
    bd_width = f_bd.shape[1]
    block = (a_width * c_width // n_pb, bd_width)
    eye = jnp.eye(Q_GROUP, dtype=t1.dtype)
    singles = jnp.einsum("qr,ka->qark", eye, t1).reshape(Q_GROUP * a_width, Q_GROUP * n_occ)
    q_step = n_q // Q_STEPS
    return pl.pallas_call(
        contract_kernel,
        grid=(Q_STEPS,),
        out_shape=[jax.ShapeDtypeStruct(block, jnp.bfloat16)] * n_pb,
        in_specs=[
            SMEM,
            pl.BlockSpec((q_step, a_width, c_width), lambda step: (step, 0, 0)),
            pl.BlockSpec((q_step, n_occ, c_width), lambda step: (step, 0, 0)),
            pl.BlockSpec(singles.shape, lambda step: (0, 0)),
            pl.BlockSpec(f_bd.shape, lambda step: (0, 0)),
        ],
        out_specs=[pl.BlockSpec(memory_space=pl.ANY)] * n_pb,
        scratch_shapes=[
            pltpu.VMEM((c_width // LANES, n_q * a_width, LANES), jnp.float32),
            pltpu.VMEM((n_pb, *block), jnp.bfloat16),
            pltpu.SemaphoreType.DMA((n_pb,)),
        ],
        cost_estimate=pl.CostEstimate(
            flops=2 * n_q * a_width * c_width * bd_width, bytes_accessed=7 << 20, transcendentals=0
        ),
    )(place, b_ac, b_oc, singles, f_bd)


def merge_kernel(core_ref, up_ref, down_ref, across_ref, up2_ref, down2_ref, up_out, down_out):
    across = across_ref[...].astype(jnp.float32)
    zero = jnp.zeros_like(across)
    for core, passing_ref, own_ref, out_ref in (
        (0, up_ref, up2_ref, up_out),
        (1, down_ref, down2_ref, down_out),
    ):
        total = own_ref[...].astype(jnp.float32) + passing_ref[...].astype(jnp.float32)
        total += jnp.where(core_ref[0] == core, across, zero)
        out_ref[...] = total.astype(out_ref.dtype)


def merge(core, up, down, across, up2, down2):
    return pl.pallas_call(
        merge_kernel,
        out_shape=[jax.ShapeDtypeStruct(up2.shape, up2.dtype)] * 2,
        in_specs=[SMEM] + [VMEM] * 5,
        out_specs=[VMEM] * 2,
        cost_estimate=pl.CostEstimate(flops=4 * up2.size, bytes_accessed=2 << 20, transcendentals=0),
    )(core, up, down, across, up2, down2)


def combine_kernel(
    own_ref, up_ref, down_ref, up2_ref, down2_ref, t2_ref, out_ref, ladder_ref, turned_ref, factor_ref
):
    total = own_ref[...].astype(jnp.float32)
    total += up_ref[...].astype(jnp.float32)
    total += down_ref[...].astype(jnp.float32)
    total += up2_ref[...].astype(jnp.float32)
    total += down2_ref[...].astype(jnp.float32)
    for b_high in range(BB // LANE_GROUPS):
        ladder_ref[b_high] = total[:, b_high * LANES : (b_high + 1) * LANES]
    n_rows = total.shape[0] // LANE_GROUPS
    group = lax.broadcasted_iota(jnp.int32, (n_rows, LANES), 1) // DB

    def pick(by_group):
        chosen = by_group[0]
        for lane_group in range(1, LANE_GROUPS):
            chosen = jnp.where(group == lane_group, by_group[lane_group], chosen)
        return chosen

    for b_high in range(BB // LANE_GROUPS):
        by_c = [
            ladder_ref.at[b_high][pl.ds(c_low, n_rows, stride=LANE_GROUPS), :]
            for c_low in range(LANE_GROUPS)
        ]
        skewed = []
        for turn in range(LANE_GROUPS):
            mixed = pick([by_c[(b_low + turn) % LANE_GROUPS] for b_low in range(LANE_GROUPS)])
            skewed.append(pltpu.roll(mixed, turn * DB, 1) if turn else mixed)
        for b_low in range(LANE_GROUPS):
            b = b_high * LANE_GROUPS + b_low
            by_b = pick([skewed[(c_low - b_low) % LANE_GROUPS] for c_low in range(LANE_GROUPS)])
            for a in range(n_rows // BB):
                at = (a * BB + b) * BB
                turned_ref[at : at + BB, :] = by_b[a * BB : (a + 1) * BB]
    for c_high in range(BB):
        tile = turned_ref[pl.ds(c_high, n_rows, stride=BB), :]
        factor_ref[:, c_high * LANES : (c_high + 1) * LANES] = tile.astype(jnp.bfloat16)
    out_ref[...] = lax.dot_general(
        t2_ref[...],
        factor_ref[...],
        (((1,), (1,)), ((), ())),
        preferred_element_type=jnp.float32,
    )


def combine(parts, t2):
    block_rows, bd_width = parts[0].shape
    pairs, cd_width = t2.shape
    ab_width = block_rows * bd_width // cd_width
    return pl.pallas_call(
        combine_kernel,
        out_shape=jax.ShapeDtypeStruct((pairs, ab_width), jnp.float32),
        in_specs=[VMEM] * 6,
        out_specs=VMEM,
        scratch_shapes=[
            pltpu.VMEM((BB // LANE_GROUPS, block_rows, LANES), jnp.float32),
            pltpu.VMEM((ab_width * BB, LANES), jnp.float32),
            pltpu.VMEM((ab_width, cd_width), jnp.bfloat16),
        ],
        cost_estimate=pl.CostEstimate(
            flops=2 * pairs * ab_width * cd_width, bytes_accessed=3 << 20, transcendentals=0
        ),
    )(*parts, t2)


def along_pb(array, distance):
    n_pb = lax.axis_size("pb")
    return lax.ppermute(array, "pb", [(y, (y + distance) % n_pb) for y in range(n_pb)])


def across_pb(array, distance):
    n_pb = lax.axis_size("pb")
    pairs = []
    for col in range(lax.axis_size("col")):
        way = -distance if col % 2 else distance
        pairs += [(col * n_pb + y, col * n_pb + (y + way) % n_pb) for y in range(n_pb)]
    return lax.ppermute(array, ("col", "pb"), pairs)


def step(b_ac, b_oc, t1, f_bd, t2):
    n_aa = lax.axis_size("aa")
    n_pb = lax.axis_size("pb")
    n_out = lax.axis_size("col") * n_pb
    place = lax.axis_index("pb").astype(jnp.int32).reshape(1)
    core = lax.rem(lax.axis_index("col"), 2).astype(jnp.int32).reshape(1)

    amplitudes = lax.all_to_all(
        jnp.broadcast_to(t2[None], (n_aa, *t2.shape)), "aa", 0, 0, tiled=True
    ).reshape(-1, t2.shape[1])

    own, up1, up2, up3, across, down3, down2, down1 = contract(b_ac, b_oc, t1, f_bd, place, n_pb)
    across = across_pb(across, 2)
    up3 = along_pb(up3, 1)
    down3 = along_pb(down3, -1)
    up1 = along_pb(up1, 1)
    down1 = along_pb(down1, -1)
    up2, down2 = merge(core, up3, down3, across, up2, down2)
    up2 = along_pb(up2, 2)
    down2 = along_pb(down2, -2)
    *parts, amplitudes = lax.optimization_barrier((own, up1, down1, up2, down2, amplitudes))
    sums = combine(parts, amplitudes)
    shares = sums.reshape(n_out, -1, sums.shape[1])
    shares = lax.all_to_all(shares, ("col", "pb"), 0, 0, tiled=True)
    return jnp.sum(shares, axis=0)


def solution(mesh):
    placed = (
        P("pb", "aa", "col"),
        P("pb", None, "col"),
        P(None, "aa"),
        P("pb", None),
        P("aa", ("col", "pb")),
    )
    return jax.shard_map(
        step, mesh=mesh, in_specs=placed, out_specs=P(("col", "pb"), "aa"), check_vma=False
    )
```

```python
import jax
import jax.numpy as jnp
from jax import lax
from jax.experimental import pallas as pl
from jax.experimental.pallas import tpu as pltpu
from jax.sharding import PartitionSpec as P


BB = 8
DB = 32
LANES = 128
LANE_GROUPS = LANES // DB
Q_GROUP = 8
Q_STEPS = 4
VMEM = pl.BlockSpec(memory_space=pltpu.VMEM)
SMEM = pl.BlockSpec(memory_space=pltpu.SMEM)


def contract_kernel(place_ref, b_ac_ref, b_oc_ref, singles_ref, f_ref, *refs):
    out_refs, (dressed_ref, ladder_ref, sems) = refs[:-3], refs[-3:]
    n_q, a_width, c_width = b_ac_ref.shape
    n_total = dressed_ref.shape[1] // a_width
    n_pb, block_rows, _ = ladder_ref.shape
    c_block = block_rows // a_width
    size = Q_GROUP * a_width
    step = pl.program_id(0)
    for group in range(n_q // Q_GROUP):
        rows = slice(group * Q_GROUP, (group + 1) * Q_GROUP)
        occupied = b_oc_ref[rows].reshape(-1, c_width)
        correction = jnp.dot(singles_ref[...], occupied, preferred_element_type=jnp.float32)
        block = b_ac_ref[rows].reshape(size, c_width).astype(jnp.float32)
        dressed = (block - correction).astype(jnp.bfloat16).astype(jnp.float32)
        at = pl.ds(pl.multiple_of((step * (n_q // Q_GROUP) + group) * size, size), size)
        for half in range(c_width // LANES):
            dressed_ref[half, at, :] = dressed[:, half * LANES : (half + 1) * LANES]

    @pl.when(step == pl.num_programs(0) - 1)
    def _():
        factors = f_ref[...]
        for half in range(c_width // LANES):
            for a in range(a_width):
                slab = dressed_ref.at[half][pl.ds(a, n_total, stride=a_width), :]
                part = lax.dot_general(
                    slab.astype(jnp.bfloat16),
                    factors,
                    (((0,), (0,)), ((), ())),
                    preferred_element_type=jnp.float32,
                ).astype(ladder_ref.dtype)
                for c_at in range(0, LANES, c_block):
                    ladder_ref[(half * LANES + c_at) // c_block, a * c_block : (a + 1) * c_block, :] = (
                        part[c_at : c_at + c_block]
                    )
        own_ref, up_ref, up2_ref, across_ref, down2_ref, down_ref = out_refs
        by_distance = (
            own_ref,
            up_ref.at[0],
            up2_ref,
            up_ref.at[1],
            across_ref,
            down_ref.at[1],
            down2_ref,
            down_ref.at[0],
        )
        copies = [
            pltpu.make_async_copy(
                ladder_ref.at[lax.rem(place_ref[0] + distance, n_pb)], out_ref, sems.at[distance]
            )
            for distance, out_ref in enumerate(by_distance)
        ]
        for copy in copies:
            copy.start()
        for copy in copies:
            copy.wait()


def contract(b_ac, b_oc, t1, f_bd, place, n_pb):
    n_q, a_width, c_width = b_ac.shape
    n_occ = b_oc.shape[1]
    bd_width = f_bd.shape[1]
    block = (a_width * c_width // n_pb, bd_width)
    pair = (2, *block)
    shapes = (block, pair, block, block, block, pair)
    eye = jnp.eye(Q_GROUP, dtype=t1.dtype)
    singles = jnp.einsum("qr,ka->qark", eye, t1).reshape(Q_GROUP * a_width, Q_GROUP * n_occ)
    q_step = n_q // Q_STEPS
    return pl.pallas_call(
        contract_kernel,
        grid=(Q_STEPS,),
        out_shape=[jax.ShapeDtypeStruct(shape, jnp.bfloat16) for shape in shapes],
        in_specs=[
            SMEM,
            pl.BlockSpec((q_step, a_width, c_width), lambda step: (step, 0, 0)),
            pl.BlockSpec((q_step, n_occ, c_width), lambda step: (step, 0, 0)),
            pl.BlockSpec(singles.shape, lambda step: (0, 0)),
            pl.BlockSpec(f_bd.shape, lambda step: (0, 0)),
        ],
        out_specs=[pl.BlockSpec(memory_space=pl.ANY)] * len(shapes),
        scratch_shapes=[
            pltpu.VMEM((c_width // LANES, n_q * a_width, LANES), jnp.float32),
            pltpu.VMEM((n_pb, *block), jnp.bfloat16),
            pltpu.SemaphoreType.DMA((n_pb,)),
        ],
        cost_estimate=pl.CostEstimate(
            flops=2 * n_q * a_width * c_width * bd_width, bytes_accessed=7 << 20, transcendentals=0
        ),
    )(place, b_ac, b_oc, singles, f_bd)


def merge_kernel(core_ref, up_ref, down_ref, across_ref, up2_ref, down2_ref, up_out, down_out):
    across = across_ref[...].astype(jnp.float32)
    zero = jnp.zeros_like(across)
    for core, passing_ref, own_ref, out_ref in (
        (0, up_ref, up2_ref, up_out),
        (1, down_ref, down2_ref, down_out),
    ):
        total = own_ref[...].astype(jnp.float32) + passing_ref[1].astype(jnp.float32)
        total += jnp.where(core_ref[0] == core, across, zero)
        out_ref[...] = total.astype(out_ref.dtype)


def merge(core, up, down, across, up2, down2):
    return pl.pallas_call(
        merge_kernel,
        out_shape=[jax.ShapeDtypeStruct(up2.shape, up2.dtype)] * 2,
        in_specs=[SMEM] + [VMEM] * 5,
        out_specs=[VMEM] * 2,
        compiler_params=pltpu.CompilerParams(vmem_limit_bytes=8 << 20),
        cost_estimate=pl.CostEstimate(flops=4 * up2.size, bytes_accessed=2 << 20, transcendentals=0),
    )(core, up, down, across, up2, down2)


def combine_kernel(
    own_ref, up_ref, down_ref, up2_ref, down2_ref, t2_ref, out_ref, ladder_ref, turned_ref, *factor_refs
):
    total = own_ref[...].astype(jnp.float32)
    total += up_ref[0].astype(jnp.float32)
    total += down_ref[0].astype(jnp.float32)
    total += up2_ref[...].astype(jnp.float32)
    total += down2_ref[...].astype(jnp.float32)
    for b_high in range(BB // LANE_GROUPS):
        ladder_ref[b_high] = total[:, b_high * LANES : (b_high + 1) * LANES]
    n_rows = total.shape[0] // LANE_GROUPS
    group = lax.broadcasted_iota(jnp.int32, (n_rows, LANES), 1) // DB

    def pick(by_group):
        chosen = by_group[0]
        for lane_group in range(1, LANE_GROUPS):
            chosen = jnp.where(group == lane_group, by_group[lane_group], chosen)
        return chosen

    for b_high in range(BB // LANE_GROUPS):
        by_c = [
            ladder_ref.at[b_high][pl.ds(c_low, n_rows, stride=LANE_GROUPS), :]
            for c_low in range(LANE_GROUPS)
        ]
        skewed = []
        for turn in range(LANE_GROUPS):
            mixed = pick([by_c[(b_low + turn) % LANE_GROUPS] for b_low in range(LANE_GROUPS)])
            skewed.append(pltpu.roll(mixed, turn * DB, 1) if turn else mixed)
        for b_low in range(LANE_GROUPS):
            b = b_high * LANE_GROUPS + b_low
            by_b = pick([skewed[(c_low - b_low) % LANE_GROUPS] for c_low in range(LANE_GROUPS)])
            for a in range(n_rows // BB):
                at = (a * BB + b) * BB
                turned_ref[at : at + BB, :] = by_b[a * BB : (a + 1) * BB]
    for c_high in range(BB):
        tile = turned_ref[pl.ds(c_high, n_rows, stride=BB), :]
        high = tile.astype(jnp.bfloat16)
        low = (tile - high.astype(jnp.float32)).astype(jnp.bfloat16)
        for factor_ref, factor in zip(factor_refs, (high, low)):
            factor_ref[:, c_high * LANES : (c_high + 1) * LANES] = factor
    sums = [
        lax.dot_general(
            t2_ref[...],
            factor_ref[...],
            (((1,), (1,)), ((), ())),
            preferred_element_type=jnp.float32,
        )
        for factor_ref in factor_refs
    ]
    out_ref[...] = (sums[0] + sums[1]).astype(out_ref.dtype)


def combine(parts, t2):
    block_rows, bd_width = parts[0].shape
    pairs, cd_width = t2.shape
    ab_width = block_rows * bd_width // cd_width
    return pl.pallas_call(
        combine_kernel,
        out_shape=jax.ShapeDtypeStruct((pairs, ab_width), jnp.bfloat16),
        in_specs=[VMEM] * 6,
        out_specs=VMEM,
        scratch_shapes=[
            pltpu.VMEM((BB // LANE_GROUPS, block_rows, LANES), jnp.float32),
            pltpu.VMEM((ab_width * BB, LANES), jnp.float32),
            pltpu.VMEM((ab_width, cd_width), jnp.bfloat16),
            pltpu.VMEM((ab_width, cd_width), jnp.bfloat16),
        ],
        compiler_params=pltpu.CompilerParams(vmem_limit_bytes=16 << 20),
        cost_estimate=pl.CostEstimate(
            flops=2 * pairs * ab_width * cd_width, bytes_accessed=3 << 20, transcendentals=0
        ),
    )(*parts, t2)


def along_pb(array, distance):
    n_pb = lax.axis_size("pb")
    return lax.ppermute(array, "pb", [(y, (y + distance) % n_pb) for y in range(n_pb)])


def across_pb(array, distance):
    n_pb = lax.axis_size("pb")
    pairs = []
    for col in range(lax.axis_size("col")):
        way = -distance if col % 2 else distance
        pairs += [(col * n_pb + y, col * n_pb + (y + way) % n_pb) for y in range(n_pb)]
    return lax.ppermute(array, ("col", "pb"), pairs)


def step(b_ac, b_oc, t1, f_bd, t2):
    n_aa = lax.axis_size("aa")
    n_pb = lax.axis_size("pb")
    n_out = lax.axis_size("col") * n_pb
    place = lax.axis_index("pb").astype(jnp.int32).reshape(1)
    core = lax.rem(lax.axis_index("col"), 2).astype(jnp.int32).reshape(1)

    amplitudes = lax.all_to_all(
        jnp.broadcast_to(t2[None], (n_aa, *t2.shape)), "aa", 0, 0, tiled=True
    ).reshape(-1, t2.shape[1])

    own, up, up2, across, down2, down = contract(b_ac, b_oc, t1, f_bd, place, n_pb)
    up = along_pb(up, 1)
    down = along_pb(down, -1)
    across = across_pb(across, 2)
    up2, down2 = merge(core, up, down, across, up2, down2)
    up2 = along_pb(up2, 2)
    down2 = along_pb(down2, -2)
    *parts, amplitudes = lax.optimization_barrier((own, up, down, up2, down2, amplitudes))
    sums = combine(parts, amplitudes)
    shares = sums.reshape(n_out, -1, sums.shape[1])
    shares = lax.all_to_all(shares, ("col", "pb"), 0, 0, tiled=True)
    return jnp.sum(shares.astype(jnp.float32), axis=0)


def solution(mesh):
    placed = (
        P("pb", "aa", "col"),
        P("pb", None, "col"),
        P(None, "aa"),
        P("pb", None),
        P("aa", ("col", "pb")),
    )
    return jax.shard_map(
        step, mesh=mesh, in_specs=placed, out_specs=P(("col", "pb"), "aa"), check_vma=False
    )
```

```python
import jax
import jax.numpy as jnp
from jax import lax
from jax.experimental import pallas as pl
from jax.experimental.pallas import tpu as pltpu
from jax.sharding import PartitionSpec as P


BB = 8
DB = 32
LANES = 128
LANE_GROUPS = LANES // DB
Q_GROUP = 8
Q_STEPS = 6
VMEM = pl.BlockSpec(memory_space=pltpu.VMEM)
SMEM = pl.BlockSpec(memory_space=pltpu.SMEM)


def contract_kernel(place_ref, b_ac_ref, b_oc_ref, t1_ref, f_ref, *refs):
    out_refs, (singles_ref, dressed_ref, ladder_ref, sems) = refs[:-4], refs[-4:]
    n_q, a_width, c_width = b_ac_ref.shape
    n_total = dressed_ref.shape[1] // a_width
    n_pb, block_rows, _ = ladder_ref.shape
    c_block = block_rows // a_width
    size = Q_GROUP * a_width
    step = pl.program_id(0)

    @pl.when(step == 0)
    def _():
        n_occ = b_oc_ref.shape[1]
        row = lax.broadcasted_iota(jnp.int32, (size, a_width), 0)
        column = lax.broadcasted_iota(jnp.int32, (size, a_width), 1)
        tall = jnp.where(row % a_width == column, 1.0, 0.0).astype(jnp.bfloat16)
        row = lax.broadcasted_iota(jnp.int32, (n_occ, Q_GROUP * n_occ), 0)
        column = lax.broadcasted_iota(jnp.int32, (n_occ, Q_GROUP * n_occ), 1)
        wide = jnp.where(column % n_occ == row, 1.0, 0.0).astype(jnp.bfloat16)
        rows = jnp.dot(tall, t1_ref[...], preferred_element_type=jnp.float32).astype(jnp.bfloat16)
        repeated = jnp.dot(rows, wide, preferred_element_type=jnp.float32)
        row = lax.broadcasted_iota(jnp.int32, repeated.shape, 0)
        column = lax.broadcasted_iota(jnp.int32, repeated.shape, 1)
        same = row // a_width == column // n_occ
        singles_ref[...] = jnp.where(same, repeated, 0.0).astype(jnp.bfloat16)

    for group in range(n_q // Q_GROUP):
        rows = slice(group * Q_GROUP, (group + 1) * Q_GROUP)
        occupied = b_oc_ref[rows].reshape(-1, c_width)
        correction = jnp.dot(singles_ref[...], occupied, preferred_element_type=jnp.float32)
        block = b_ac_ref[rows].reshape(size, c_width).astype(jnp.float32)
        dressed = (block - correction).astype(jnp.bfloat16).astype(jnp.float32)
        at = pl.ds(pl.multiple_of((step * (n_q // Q_GROUP) + group) * size, size), size)
        for half in range(c_width // LANES):
            dressed_ref[half, at, :] = dressed[:, half * LANES : (half + 1) * LANES]

    @pl.when(step == pl.num_programs(0) - 1)
    def _():
        factors = f_ref[...]
        for half in range(c_width // LANES):
            for a in range(a_width):
                slab = dressed_ref.at[half][pl.ds(a, n_total, stride=a_width), :]
                part = lax.dot_general(
                    slab.astype(jnp.bfloat16),
                    factors,
                    (((0,), (0,)), ((), ())),
                    preferred_element_type=jnp.float32,
                ).astype(ladder_ref.dtype)
                for c_at in range(0, LANES, c_block):
                    ladder_ref[(half * LANES + c_at) // c_block, a * c_block : (a + 1) * c_block, :] = (
                        part[c_at : c_at + c_block]
                    )
        own_ref, up_ref, up2_ref, across_ref, down2_ref, down_ref = out_refs
        by_distance = (
            own_ref,
            up_ref.at[0],
            up2_ref,
            up_ref.at[1],
            across_ref,
            down_ref.at[1],
            down2_ref,
            down_ref.at[0],
        )
        copies = [
            pltpu.make_async_copy(
                ladder_ref.at[lax.rem(place_ref[0] + distance, n_pb)], out_ref, sems.at[distance]
            )
            for distance, out_ref in enumerate(by_distance)
        ]
        for copy in copies:
            copy.start()
        for copy in copies:
            copy.wait()


def contract(b_ac, b_oc, t1, f_bd, place, n_pb):
    n_q, a_width, c_width = b_ac.shape
    n_occ = b_oc.shape[1]
    bd_width = f_bd.shape[1]
    block = (a_width * c_width // n_pb, bd_width)
    pair = (2, *block)
    shapes = (block, pair, block, block, block, pair)
    q_step = n_q // Q_STEPS
    return pl.pallas_call(
        contract_kernel,
        grid=(Q_STEPS,),
        out_shape=[jax.ShapeDtypeStruct(shape, jnp.bfloat16) for shape in shapes],
        in_specs=[
            SMEM,
            pl.BlockSpec((q_step, a_width, c_width), lambda step: (step, 0, 0)),
            pl.BlockSpec((q_step, n_occ, c_width), lambda step: (step, 0, 0)),
            pl.BlockSpec((a_width, n_occ), lambda step: (0, 0)),
            pl.BlockSpec(f_bd.shape, lambda step: (0, 0)),
        ],
        out_specs=[pl.BlockSpec(memory_space=pl.ANY)] * len(shapes),
        scratch_shapes=[
            pltpu.VMEM((Q_GROUP * a_width, Q_GROUP * n_occ), jnp.bfloat16),
            pltpu.VMEM((c_width // LANES, n_q * a_width, LANES), jnp.float32),
            pltpu.VMEM((n_pb, *block), jnp.bfloat16),
            pltpu.SemaphoreType.DMA((n_pb,)),
        ],
        cost_estimate=pl.CostEstimate(
            flops=2 * n_q * a_width * c_width * bd_width, bytes_accessed=7 << 20, transcendentals=0
        ),
    )(place, b_ac, b_oc, t1.T, f_bd)


def merge_kernel(up_ref, down_ref, up2_ref, down2_ref, up_out, down_out):
    for passing_ref, own_ref, out_ref in (
        (up_ref, up2_ref, up_out),
        (down_ref, down2_ref, down_out),
    ):
        total = own_ref[...].astype(jnp.float32) + passing_ref[1].astype(jnp.float32)
        out_ref[...] = total.astype(out_ref.dtype)


def merge(up, down, up2, down2):
    return pl.pallas_call(
        merge_kernel,
        out_shape=[jax.ShapeDtypeStruct(up2.shape, up2.dtype)] * 2,
        in_specs=[VMEM] * 4,
        out_specs=[VMEM] * 2,
        compiler_params=pltpu.CompilerParams(vmem_limit_bytes=8 << 20),
        cost_estimate=pl.CostEstimate(flops=2 * up2.size, bytes_accessed=2 << 20, transcendentals=0),
    )(up, down, up2, down2)


def combine_kernel(
    own_ref, across_ref, up_ref, down_ref, up2_ref, down2_ref, t2_ref, out_ref, ladder_ref, turned_ref, *factor_refs
):
    total = own_ref[...].astype(jnp.float32)
    total += across_ref[...].astype(jnp.float32)
    total += up_ref[0].astype(jnp.float32)
    total += down_ref[0].astype(jnp.float32)
    total += up2_ref[...].astype(jnp.float32)
    total += down2_ref[...].astype(jnp.float32)
    for b_high in range(BB // LANE_GROUPS):
        ladder_ref[b_high] = total[:, b_high * LANES : (b_high + 1) * LANES]
    n_rows = total.shape[0] // LANE_GROUPS
    group = lax.broadcasted_iota(jnp.int32, (n_rows, LANES), 1) // DB

    def pick(by_group):
        chosen = by_group[0]
        for lane_group in range(1, LANE_GROUPS):
            chosen = jnp.where(group == lane_group, by_group[lane_group], chosen)
        return chosen

    for b_high in range(BB // LANE_GROUPS):
        by_c = [
            ladder_ref.at[b_high][pl.ds(c_low, n_rows, stride=LANE_GROUPS), :]
            for c_low in range(LANE_GROUPS)
        ]
        skewed = []
        for turn in range(LANE_GROUPS):
            mixed = pick([by_c[(b_low + turn) % LANE_GROUPS] for b_low in range(LANE_GROUPS)])
            skewed.append(pltpu.roll(mixed, turn * DB, 1) if turn else mixed)
        for b_low in range(LANE_GROUPS):
            b = b_high * LANE_GROUPS + b_low
            by_b = pick([skewed[(c_low - b_low) % LANE_GROUPS] for c_low in range(LANE_GROUPS)])
            for a in range(n_rows // BB):
                at = (a * BB + b) * BB
                turned_ref[at : at + BB, :] = by_b[a * BB : (a + 1) * BB]
    for c_high in range(BB):
        tile = turned_ref[pl.ds(c_high, n_rows, stride=BB), :]
        high = tile.astype(jnp.bfloat16)
        low = (tile - high.astype(jnp.float32)).astype(jnp.bfloat16)
        for factor_ref, factor in zip(factor_refs, (high, low)):
            factor_ref[:, c_high * LANES : (c_high + 1) * LANES] = factor
    sums = [
        lax.dot_general(
            t2_ref[...],
            factor_ref[...],
            (((1,), (1,)), ((), ())),
            preferred_element_type=jnp.float32,
        )
        for factor_ref in factor_refs
    ]
    out_ref[...] = (sums[0] + sums[1]).astype(out_ref.dtype)


def combine(parts, t2):
    block_rows, bd_width = parts[0].shape
    pairs, cd_width = t2.shape
    ab_width = block_rows * bd_width // cd_width
    return pl.pallas_call(
        combine_kernel,
        out_shape=jax.ShapeDtypeStruct((pairs, ab_width), jnp.bfloat16),
        in_specs=[VMEM] * (len(parts) + 1),
        out_specs=VMEM,
        scratch_shapes=[
            pltpu.VMEM((BB // LANE_GROUPS, block_rows, LANES), jnp.float32),
            pltpu.VMEM((ab_width * BB, LANES), jnp.float32),
            pltpu.VMEM((ab_width, cd_width), jnp.bfloat16),
            pltpu.VMEM((ab_width, cd_width), jnp.bfloat16),
        ],
        compiler_params=pltpu.CompilerParams(vmem_limit_bytes=16 << 20),
        cost_estimate=pl.CostEstimate(
            flops=2 * pairs * ab_width * cd_width, bytes_accessed=3 << 20, transcendentals=0
        ),
    )(*parts, t2)


def along_pb(array, distance):
    n_pb = lax.axis_size("pb")
    return lax.ppermute(array, "pb", [(y, (y + distance) % n_pb) for y in range(n_pb)])


def across_pb(array, distance):
    n_pb = lax.axis_size("pb")
    pairs = []
    for col in range(lax.axis_size("col")):
        way = -distance if col % 2 else distance
        pairs += [(col * n_pb + y, col * n_pb + (y + way) % n_pb) for y in range(n_pb)]
    return lax.ppermute(array, ("col", "pb"), pairs)


def step(b_ac, b_oc, t1, f_bd, t2):
    n_aa = lax.axis_size("aa")
    n_pb = lax.axis_size("pb")
    n_out = lax.axis_size("col") * n_pb
    place = lax.axis_index("pb").astype(jnp.int32).reshape(1)

    amplitudes = lax.all_to_all(
        jnp.broadcast_to(t2[None], (n_aa, *t2.shape)), "aa", 0, 0, tiled=True
    ).reshape(-1, t2.shape[1])

    own, up, up2, across, down2, down = contract(b_ac, b_oc, t1, f_bd, place, n_pb)
    up = along_pb(up, 1)
    down = along_pb(down, -1)
    across = across_pb(across, 4)
    up2, down2 = merge(up, down, up2, down2)
    up2 = along_pb(up2, 2)
    down2 = along_pb(down2, -2)
    *parts, amplitudes = lax.optimization_barrier(
        (own, across, up, down, up2, down2, amplitudes)
    )
    sums = combine(parts, amplitudes)
    shares = sums.reshape(n_out, -1, sums.shape[1])
    shares = lax.all_to_all(shares, ("col", "pb"), 0, 0, tiled=True)
    return jnp.sum(shares.astype(jnp.float32), axis=0)


def solution(mesh):
    placed = (
        P("pb", "aa", "col"),
        P("pb", None, "col"),
        P(None, "aa"),
        P("pb", None),
        P("aa", ("col", "pb")),
    )
    return jax.shard_map(
        step, mesh=mesh, in_specs=placed, out_specs=P(("col", "pb"), "aa"), check_vma=False
    )
```

```python
import jax
import jax.numpy as jnp
from jax import lax
from jax.experimental import pallas as pl
from jax.experimental.pallas import tpu as pltpu
from jax.sharding import PartitionSpec as P


BB = 8
DB = 32
LANES = 128
LANE_GROUPS = LANES // DB
Q_GROUP = 8
Q_STEPS = 6
A_CHUNK = 4
VMEM = pl.BlockSpec(memory_space=pltpu.VMEM)
SMEM = pl.BlockSpec(memory_space=pltpu.SMEM)


def contract_kernel(place_ref, b_ac_ref, b_oc_ref, t1_ref, f_ref, t2_ref, *refs):
    out_refs, (singles_ref, dressed_ref, ladder_ref, sems, t2_sems) = refs[:-5], refs[-5:]
    own_ref, up_ref, up2_ref, across_ref, down2_ref, down_ref, repeats_ref = out_refs
    n_q, a_width, c_width = b_ac_ref.shape
    n_total = dressed_ref.shape[1] // a_width
    n_pb, block_rows, _ = ladder_ref.shape
    c_block = block_rows // a_width
    size = Q_GROUP * a_width
    step = pl.program_id(0)
    repeats = [
        pltpu.make_async_copy(t2_ref, repeats_ref.at[at], t2_sems.at[at])
        for at in range(repeats_ref.shape[0])
    ]

    @pl.when(step == 0)
    def _():
        for copy in repeats:
            copy.start()
        n_occ = b_oc_ref.shape[1]
        row = lax.broadcasted_iota(jnp.int32, (size, a_width), 0)
        column = lax.broadcasted_iota(jnp.int32, (size, a_width), 1)
        tall = jnp.where(row % a_width == column, 1.0, 0.0).astype(jnp.bfloat16)
        row = lax.broadcasted_iota(jnp.int32, (n_occ, Q_GROUP * n_occ), 0)
        column = lax.broadcasted_iota(jnp.int32, (n_occ, Q_GROUP * n_occ), 1)
        wide = jnp.where(column % n_occ == row, 1.0, 0.0).astype(jnp.bfloat16)
        rows = jnp.dot(tall, t1_ref[...], preferred_element_type=jnp.float32).astype(jnp.bfloat16)
        repeated = jnp.dot(rows, wide, preferred_element_type=jnp.float32)
        row = lax.broadcasted_iota(jnp.int32, repeated.shape, 0)
        column = lax.broadcasted_iota(jnp.int32, repeated.shape, 1)
        same = row // a_width == column // n_occ
        singles_ref[...] = jnp.where(same, repeated, 0.0).astype(jnp.bfloat16)

    for group in range(n_q // Q_GROUP):
        rows = slice(group * Q_GROUP, (group + 1) * Q_GROUP)
        occupied = b_oc_ref[rows].reshape(-1, c_width)
        correction = jnp.dot(singles_ref[...], occupied, preferred_element_type=jnp.float32)
        block = b_ac_ref[rows].reshape(size, c_width).astype(jnp.float32)
        dressed = (block - correction).astype(jnp.bfloat16).astype(jnp.float32)
        at = pl.ds(pl.multiple_of((step * (n_q // Q_GROUP) + group) * size, size), size)
        for half in range(c_width // LANES):
            dressed_ref[half, at, :] = dressed[:, half * LANES : (half + 1) * LANES]

    @pl.when(step == pl.num_programs(0) - 1)
    def _():
        factors = f_ref[...]
        by_distance = (
            own_ref,
            up_ref.at[0],
            up2_ref,
            up_ref.at[1],
            across_ref,
            down_ref.at[1],
            down2_ref,
            down_ref.at[0],
        )
        copies = []
        for a in range(a_width):
            for half in range(c_width // LANES):
                slab = dressed_ref.at[half][pl.ds(a, n_total, stride=a_width), :]
                part = lax.dot_general(
                    slab.astype(jnp.bfloat16),
                    factors,
                    (((0,), (0,)), ((), ())),
                    preferred_element_type=jnp.float32,
                ).astype(ladder_ref.dtype)
                for c_at in range(0, LANES, c_block):
                    ladder_ref[(half * LANES + c_at) // c_block, a * c_block : (a + 1) * c_block, :] = (
                        part[c_at : c_at + c_block]
                    )
            if (a + 1) % A_CHUNK == 0:
                chunk = a // A_CHUNK
                rows = pl.ds(chunk * A_CHUNK * c_block, A_CHUNK * c_block)
                for distance, out_ref in enumerate(by_distance):
                    copy = pltpu.make_async_copy(
                        ladder_ref.at[lax.rem(place_ref[0] + distance, n_pb), rows],
                        out_ref.at[rows],
                        sems.at[chunk, distance],
                    )
                    copy.start()
                    copies.append(copy)
        for copy in copies + repeats:
            copy.wait()


def contract(b_ac, b_oc, t1, f_bd, t2, place, n_pb, n_aa):
    n_q, a_width, c_width = b_ac.shape
    n_occ = b_oc.shape[1]
    bd_width = f_bd.shape[1]
    block = (a_width * c_width // n_pb, bd_width)
    pair = (2, *block)
    shapes = (block, pair, block, block, block, pair, (n_aa, *t2.shape))
    q_step = n_q // Q_STEPS
    return pl.pallas_call(
        contract_kernel,
        grid=(Q_STEPS,),
        out_shape=[jax.ShapeDtypeStruct(shape, jnp.bfloat16) for shape in shapes],
        in_specs=[
            SMEM,
            pl.BlockSpec((q_step, a_width, c_width), lambda step: (step, 0, 0)),
            pl.BlockSpec((q_step, n_occ, c_width), lambda step: (step, 0, 0)),
            pl.BlockSpec((a_width, n_occ), lambda step: (0, 0)),
            pl.BlockSpec(f_bd.shape, lambda step: (0, 0)),
            pl.BlockSpec(t2.shape, lambda step: (0, 0)),
        ],
        out_specs=[pl.BlockSpec(memory_space=pl.ANY)] * len(shapes),
        scratch_shapes=[
            pltpu.VMEM((Q_GROUP * a_width, Q_GROUP * n_occ), jnp.bfloat16),
            pltpu.VMEM((c_width // LANES, n_q * a_width, LANES), jnp.float32),
            pltpu.VMEM((n_pb, *block), jnp.bfloat16),
            pltpu.SemaphoreType.DMA((a_width // A_CHUNK, n_pb)),
            pltpu.SemaphoreType.DMA((n_aa,)),
        ],
        cost_estimate=pl.CostEstimate(
            flops=2 * n_q * a_width * c_width * bd_width, bytes_accessed=7 << 20, transcendentals=0
        ),
    )(place, b_ac, b_oc, t1.T, f_bd, t2)


def merge_kernel(core_ref, up_ref, down_ref, across_ref, up2_ref, down2_ref, up_out, down_out):
    across = across_ref[...].astype(jnp.float32)
    zero = jnp.zeros_like(across)
    for core, passing_ref, own_ref, out_ref in (
        (0, up_ref, up2_ref, up_out),
        (1, down_ref, down2_ref, down_out),
    ):
        total = own_ref[...].astype(jnp.float32) + passing_ref[1].astype(jnp.float32)
        total += jnp.where(core_ref[0] == core, across, zero)
        out_ref[...] = total.astype(out_ref.dtype)


def merge(core, up, down, across, up2, down2):
    return pl.pallas_call(
        merge_kernel,
        out_shape=[jax.ShapeDtypeStruct(up2.shape, up2.dtype)] * 2,
        in_specs=[SMEM] + [VMEM] * 5,
        out_specs=[VMEM] * 2,
        compiler_params=pltpu.CompilerParams(vmem_limit_bytes=8 << 20),
        cost_estimate=pl.CostEstimate(flops=4 * up2.size, bytes_accessed=2 << 20, transcendentals=0),
    )(core, up, down, across, up2, down2)


def combine_kernel(
    own_ref, up_ref, down_ref, up2_ref, down2_ref, t2_ref, out_ref, ladder_ref, turned_ref, *factor_refs
):
    total = own_ref[...].astype(jnp.float32)
    total += up_ref[0].astype(jnp.float32)
    total += down_ref[0].astype(jnp.float32)
    total += up2_ref[...].astype(jnp.float32)
    total += down2_ref[...].astype(jnp.float32)
    for b_high in range(BB // LANE_GROUPS):
        ladder_ref[b_high] = total[:, b_high * LANES : (b_high + 1) * LANES]
    n_rows = total.shape[0] // LANE_GROUPS
    group = lax.broadcasted_iota(jnp.int32, (n_rows, LANES), 1) // DB

    def pick(by_group):
        chosen = by_group[0]
        for lane_group in range(1, LANE_GROUPS):
            chosen = jnp.where(group == lane_group, by_group[lane_group], chosen)
        return chosen

    for b_high in range(BB // LANE_GROUPS):
        by_c = [
            ladder_ref.at[b_high][pl.ds(c_low, n_rows, stride=LANE_GROUPS), :]
            for c_low in range(LANE_GROUPS)
        ]
        skewed = []
        for turn in range(LANE_GROUPS):
            mixed = pick([by_c[(b_low + turn) % LANE_GROUPS] for b_low in range(LANE_GROUPS)])
            skewed.append(pltpu.roll(mixed, turn * DB, 1) if turn else mixed)
        for b_low in range(LANE_GROUPS):
            b = b_high * LANE_GROUPS + b_low
            by_b = pick([skewed[(c_low - b_low) % LANE_GROUPS] for c_low in range(LANE_GROUPS)])
            for a in range(n_rows // BB):
                at = (a * BB + b) * BB
                turned_ref[at : at + BB, :] = by_b[a * BB : (a + 1) * BB]
    for c_high in range(BB):
        tile = turned_ref[pl.ds(c_high, n_rows, stride=BB), :]
        high = tile.astype(jnp.bfloat16)
        low = (tile - high.astype(jnp.float32)).astype(jnp.bfloat16)
        for factor_ref, factor in zip(factor_refs, (high, low)):
            factor_ref[:, c_high * LANES : (c_high + 1) * LANES] = factor
    sums = [
        lax.dot_general(
            t2_ref[...],
            factor_ref[...],
            (((1,), (1,)), ((), ())),
            preferred_element_type=jnp.float32,
        )
        for factor_ref in factor_refs
    ]
    out_ref[...] = (sums[0] + sums[1]).astype(out_ref.dtype)


def combine(parts, t2):
    block_rows, bd_width = parts[0].shape
    pairs, cd_width = t2.shape
    ab_width = block_rows * bd_width // cd_width
    return pl.pallas_call(
        combine_kernel,
        out_shape=jax.ShapeDtypeStruct((pairs, ab_width), jnp.bfloat16),
        in_specs=[VMEM] * (len(parts) + 1),
        out_specs=VMEM,
        scratch_shapes=[
            pltpu.VMEM((BB // LANE_GROUPS, block_rows, LANES), jnp.float32),
            pltpu.VMEM((ab_width * BB, LANES), jnp.float32),
            pltpu.VMEM((ab_width, cd_width), jnp.bfloat16),
            pltpu.VMEM((ab_width, cd_width), jnp.bfloat16),
        ],
        compiler_params=pltpu.CompilerParams(vmem_limit_bytes=16 << 20),
        cost_estimate=pl.CostEstimate(
            flops=2 * pairs * ab_width * cd_width, bytes_accessed=3 << 20, transcendentals=0
        ),
    )(*parts, t2)


def along_pb(array, distance):
    n_pb = lax.axis_size("pb")
    return lax.ppermute(array, "pb", [(y, (y + distance) % n_pb) for y in range(n_pb)])


def across_pb(array, distance):
    n_pb = lax.axis_size("pb")
    pairs = []
    for col in range(lax.axis_size("col")):
        way = -distance if col % 2 else distance
        pairs += [(col * n_pb + y, col * n_pb + (y + way) % n_pb) for y in range(n_pb)]
    return lax.ppermute(array, ("col", "pb"), pairs)


def step(b_ac, b_oc, t1, f_bd, t2):
    n_aa = lax.axis_size("aa")
    n_pb = lax.axis_size("pb")
    n_out = lax.axis_size("col") * n_pb
    place = lax.axis_index("pb").astype(jnp.int32).reshape(1)
    core = lax.rem(lax.axis_index("col"), 2).astype(jnp.int32).reshape(1)

    own, up, up2, across, down2, down, repeats = contract(
        b_ac, b_oc, t1, f_bd, t2, place, n_pb, n_aa
    )
    amplitudes = lax.all_to_all(repeats, "aa", 0, 0, tiled=True).reshape(-1, t2.shape[1])
    up = along_pb(up, 1)
    down = along_pb(down, -1)
    across = across_pb(across, 2)
    up2, down2 = merge(core, up, down, across, up2, down2)
    up2 = along_pb(up2, 2)
    down2 = along_pb(down2, -2)
    *parts, amplitudes = lax.optimization_barrier((own, up, down, up2, down2, amplitudes))
    sums = combine(parts, amplitudes)
    shares = sums.reshape(n_out, -1, sums.shape[1])
    shares = lax.all_to_all(shares, ("col", "pb"), 0, 0, tiled=True)
    return jnp.sum(shares.astype(jnp.float32), axis=0)


def solution(mesh):
    placed = (
        P("pb", "aa", "col"),
        P("pb", None, "col"),
        P(None, "aa"),
        P("pb", None),
        P("aa", ("col", "pb")),
    )
    return jax.shard_map(
        step, mesh=mesh, in_specs=placed, out_specs=P(("col", "pb"), "aa"), check_vma=False
    )
```

```python
import jax
import jax.numpy as jnp
from jax import lax
from jax.experimental import pallas as pl
from jax.experimental.pallas import tpu as pltpu
from jax.sharding import PartitionSpec as P


BB = 8
DB = 32
LANES = 128
LANE_GROUPS = LANES // DB
Q_GROUP = 8
Q_STEPS = 4
A_CHUNK = 4
VMEM = pl.BlockSpec(memory_space=pltpu.VMEM)
SMEM = pl.BlockSpec(memory_space=pltpu.SMEM)


def contract_kernel(place_ref, b_ac_ref, b_oc_ref, t1_ref, f_ref, *refs):
    out_refs, (singles_ref, dressed_ref, ladder_ref, sems) = refs[:-4], refs[-4:]
    own_ref, up_ref, up2_ref, across_ref, down2_ref, down_ref = out_refs
    n_q, a_width, c_width = b_ac_ref.shape
    n_total = dressed_ref.shape[1] // a_width
    n_pb, block_rows, _ = ladder_ref.shape
    c_block = block_rows // a_width
    size = Q_GROUP * a_width
    step = pl.program_id(0)

    @pl.when(step == 0)
    def _():
        n_occ = b_oc_ref.shape[1]
        row = lax.broadcasted_iota(jnp.int32, (size, a_width), 0)
        column = lax.broadcasted_iota(jnp.int32, (size, a_width), 1)
        tall = jnp.where(row % a_width == column, 1.0, 0.0).astype(jnp.bfloat16)
        row = lax.broadcasted_iota(jnp.int32, (n_occ, Q_GROUP * n_occ), 0)
        column = lax.broadcasted_iota(jnp.int32, (n_occ, Q_GROUP * n_occ), 1)
        wide = jnp.where(column % n_occ == row, 1.0, 0.0).astype(jnp.bfloat16)
        rows = jnp.dot(tall, t1_ref[...], preferred_element_type=jnp.float32).astype(jnp.bfloat16)
        repeated = jnp.dot(rows, wide, preferred_element_type=jnp.float32)
        row = lax.broadcasted_iota(jnp.int32, repeated.shape, 0)
        column = lax.broadcasted_iota(jnp.int32, repeated.shape, 1)
        same = row // a_width == column // n_occ
        singles_ref[...] = jnp.where(same, repeated, 0.0).astype(jnp.bfloat16)

    for group in range(n_q // Q_GROUP):
        rows = slice(group * Q_GROUP, (group + 1) * Q_GROUP)
        occupied = b_oc_ref[rows].reshape(-1, c_width)
        correction = jnp.dot(singles_ref[...], occupied, preferred_element_type=jnp.float32)
        block = b_ac_ref[rows].reshape(size, c_width).astype(jnp.float32)
        dressed = (block - correction).astype(jnp.bfloat16).astype(jnp.float32)
        at = pl.ds(pl.multiple_of((step * (n_q // Q_GROUP) + group) * size, size), size)
        for half in range(c_width // LANES):
            dressed_ref[half, at, :] = dressed[:, half * LANES : (half + 1) * LANES]

    @pl.when(step == pl.num_programs(0) - 1)
    def _():
        factors = f_ref[...]
        by_distance = (
            own_ref,
            up_ref.at[0],
            up2_ref,
            up_ref.at[1],
            across_ref,
            down_ref.at[1],
            down2_ref,
            down_ref.at[0],
        )
        copies = []
        for a in range(a_width):
            for half in range(c_width // LANES):
                slab = dressed_ref.at[half][pl.ds(a, n_total, stride=a_width), :]
                part = lax.dot_general(
                    slab.astype(jnp.bfloat16),
                    factors,
                    (((0,), (0,)), ((), ())),
                    preferred_element_type=jnp.float32,
                ).astype(ladder_ref.dtype)
                for c_at in range(0, LANES, c_block):
                    ladder_ref[(half * LANES + c_at) // c_block, a * c_block : (a + 1) * c_block, :] = (
                        part[c_at : c_at + c_block]
                    )
            if (a + 1) % A_CHUNK == 0:
                chunk = a // A_CHUNK
                rows = pl.ds(chunk * A_CHUNK * c_block, A_CHUNK * c_block)
                for distance, out_ref in enumerate(by_distance):
                    copy = pltpu.make_async_copy(
                        ladder_ref.at[lax.rem(place_ref[0] + distance, n_pb), rows],
                        out_ref.at[rows],
                        sems.at[chunk, distance],
                    )
                    copy.start()
                    copies.append(copy)
        for copy in copies:
            copy.wait()


def contract(b_ac, b_oc, t1, f_bd, place, n_pb):
    n_q, a_width, c_width = b_ac.shape
    n_occ = b_oc.shape[1]
    bd_width = f_bd.shape[1]
    block = (a_width * c_width // n_pb, bd_width)
    pair = (2, *block)
    shapes = (block, pair, block, block, block, pair)
    q_step = n_q // Q_STEPS
    return pl.pallas_call(
        contract_kernel,
        grid=(Q_STEPS,),
        out_shape=[jax.ShapeDtypeStruct(shape, jnp.bfloat16) for shape in shapes],
        in_specs=[
            SMEM,
            pl.BlockSpec((q_step, a_width, c_width), lambda step: (step, 0, 0)),
            pl.BlockSpec((q_step, n_occ, c_width), lambda step: (step, 0, 0)),
            pl.BlockSpec((a_width, n_occ), lambda step: (0, 0)),
            pl.BlockSpec(f_bd.shape, lambda step: (0, 0)),
        ],
        out_specs=[pl.BlockSpec(memory_space=pl.ANY)] * len(shapes),
        scratch_shapes=[
            pltpu.VMEM((Q_GROUP * a_width, Q_GROUP * n_occ), jnp.bfloat16),
            pltpu.VMEM((c_width // LANES, n_q * a_width, LANES), jnp.float32),
            pltpu.VMEM((n_pb, *block), jnp.bfloat16),
            pltpu.SemaphoreType.DMA((a_width // A_CHUNK, n_pb)),
        ],
        cost_estimate=pl.CostEstimate(
            flops=2 * n_q * a_width * c_width * bd_width, bytes_accessed=7 << 20, transcendentals=0
        ),
    )(place, b_ac, b_oc, t1.T, f_bd)


def merge_kernel(up_ref, down_ref, up2_ref, down2_ref, up_out, down_out):
    for passing_ref, own_ref, out_ref in (
        (up_ref, up2_ref, up_out),
        (down_ref, down2_ref, down_out),
    ):
        total = own_ref[...].astype(jnp.float32) + passing_ref[1].astype(jnp.float32)
        out_ref[...] = total.astype(out_ref.dtype)


def merge(up, down, up2, down2):
    return pl.pallas_call(
        merge_kernel,
        out_shape=[jax.ShapeDtypeStruct(up2.shape, up2.dtype)] * 2,
        in_specs=[VMEM] * 4,
        out_specs=[VMEM] * 2,
        compiler_params=pltpu.CompilerParams(vmem_limit_bytes=8 << 20),
        cost_estimate=pl.CostEstimate(flops=2 * up2.size, bytes_accessed=2 << 20, transcendentals=0),
    )(up, down, up2, down2)


def combine_kernel(
    own_ref, across_ref, up_ref, down_ref, up2_ref, down2_ref, t2_ref, out_ref, ladder_ref, turned_ref, *factor_refs
):
    total = own_ref[...].astype(jnp.float32)
    total += across_ref[...].astype(jnp.float32)
    total += up_ref[0].astype(jnp.float32)
    total += down_ref[0].astype(jnp.float32)
    total += up2_ref[...].astype(jnp.float32)
    total += down2_ref[...].astype(jnp.float32)
    for b_high in range(BB // LANE_GROUPS):
        ladder_ref[b_high] = total[:, b_high * LANES : (b_high + 1) * LANES]
    n_rows = total.shape[0] // LANE_GROUPS
    group = lax.broadcasted_iota(jnp.int32, (n_rows, LANES), 1) // DB

    def pick(by_group):
        chosen = by_group[0]
        for lane_group in range(1, LANE_GROUPS):
            chosen = jnp.where(group == lane_group, by_group[lane_group], chosen)
        return chosen

    for b_high in range(BB // LANE_GROUPS):
        by_c = [
            ladder_ref.at[b_high][pl.ds(c_low, n_rows, stride=LANE_GROUPS), :]
            for c_low in range(LANE_GROUPS)
        ]
        skewed = []
        for turn in range(LANE_GROUPS):
            mixed = pick([by_c[(b_low + turn) % LANE_GROUPS] for b_low in range(LANE_GROUPS)])
            skewed.append(pltpu.roll(mixed, turn * DB, 1) if turn else mixed)
        for b_low in range(LANE_GROUPS):
            b = b_high * LANE_GROUPS + b_low
            by_b = pick([skewed[(c_low - b_low) % LANE_GROUPS] for c_low in range(LANE_GROUPS)])
            for a in range(n_rows // BB):
                at = (a * BB + b) * BB
                turned_ref[at : at + BB, :] = by_b[a * BB : (a + 1) * BB]
    for c_high in range(BB):
        tile = turned_ref[pl.ds(c_high, n_rows, stride=BB), :]
        high = tile.astype(jnp.bfloat16)
        low = (tile - high.astype(jnp.float32)).astype(jnp.bfloat16)
        for factor_ref, factor in zip(factor_refs, (high, low)):
            factor_ref[:, c_high * LANES : (c_high + 1) * LANES] = factor
    sums = [
        lax.dot_general(
            t2_ref[...],
            factor_ref[...],
            (((1,), (1,)), ((), ())),
            preferred_element_type=jnp.float32,
        )
        for factor_ref in factor_refs
    ]
    out_ref[...] = (sums[0] + sums[1]).astype(out_ref.dtype)


def combine(parts, t2):
    block_rows, bd_width = parts[0].shape
    pairs, cd_width = t2.shape
    ab_width = block_rows * bd_width // cd_width
    return pl.pallas_call(
        combine_kernel,
        out_shape=jax.ShapeDtypeStruct((pairs, ab_width), jnp.bfloat16),
        in_specs=[VMEM] * (len(parts) + 1),
        out_specs=VMEM,
        scratch_shapes=[
            pltpu.VMEM((BB // LANE_GROUPS, block_rows, LANES), jnp.float32),
            pltpu.VMEM((ab_width * BB, LANES), jnp.float32),
            pltpu.VMEM((ab_width, cd_width), jnp.bfloat16),
            pltpu.VMEM((ab_width, cd_width), jnp.bfloat16),
        ],
        compiler_params=pltpu.CompilerParams(vmem_limit_bytes=16 << 20),
        cost_estimate=pl.CostEstimate(
            flops=2 * pairs * ab_width * cd_width, bytes_accessed=3 << 20, transcendentals=0
        ),
    )(*parts, t2)


def along_pb(array, distance):
    n_pb = lax.axis_size("pb")
    return lax.ppermute(array, "pb", [(y, (y + distance) % n_pb) for y in range(n_pb)])


def across_pb(array, distance):
    n_pb = lax.axis_size("pb")
    pairs = []
    for col in range(lax.axis_size("col")):
        way = -distance if col % 2 else distance
        pairs += [(col * n_pb + y, col * n_pb + (y + way) % n_pb) for y in range(n_pb)]
    return lax.ppermute(array, ("col", "pb"), pairs)


def step(b_ac, b_oc, t1, f_bd, t2):
    n_aa = lax.axis_size("aa")
    n_pb = lax.axis_size("pb")
    n_out = lax.axis_size("col") * n_pb
    place = lax.axis_index("pb").astype(jnp.int32).reshape(1)

    amplitudes = lax.all_to_all(
        jnp.broadcast_to(t2[None], (n_aa, *t2.shape)), "aa", 0, 0, tiled=True
    ).reshape(-1, t2.shape[1])

    own, up, up2, across, down2, down = contract(b_ac, b_oc, t1, f_bd, place, n_pb)
    up = along_pb(up, 1)
    down = along_pb(down, -1)
    across = across_pb(across, 4)
    up2, down2 = merge(up, down, up2, down2)
    up2 = along_pb(up2, 2)
    down2 = along_pb(down2, -2)
    *parts, amplitudes = lax.optimization_barrier(
        (own, across, up, down, up2, down2, amplitudes)
    )
    sums = combine(parts, amplitudes)
    shares = sums.reshape(n_out, -1, sums.shape[1])
    shares = lax.all_to_all(shares, ("col", "pb"), 0, 0, tiled=True)
    return jnp.sum(shares.astype(jnp.float32), axis=0)


def solution(mesh):
    placed = (
        P("pb", "aa", "col"),
        P("pb", None, "col"),
        P(None, "aa"),
        P("pb", None),
        P("aa", ("col", "pb")),
    )
    return jax.shard_map(
        step, mesh=mesh, in_specs=placed, out_specs=P(("col", "pb"), "aa"), check_vma=False
    )
```

```python
import jax
import jax.numpy as jnp
from jax import lax
from jax.experimental import pallas as pl
from jax.experimental.pallas import tpu as pltpu
from jax.sharding import PartitionSpec as P


BB = 8
DB = 32
LANES = 128
LANE_GROUPS = LANES // DB
Q_GROUP = 8
Q_STEPS = 4
A_CHUNK = 4
VMEM = pl.BlockSpec(memory_space=pltpu.VMEM)
SMEM = pl.BlockSpec(memory_space=pltpu.SMEM)


def contract_kernel(place_ref, b_ac_ref, b_oc_ref, t1_ref, f_ref, *refs):
    out_refs, (singles_ref, dressed_ref, ladder_ref, sems) = refs[:-4], refs[-4:]
    own_ref, up_ref, up2_ref, across_ref, down2_ref, down_ref = out_refs
    n_q, a_width, c_width = b_ac_ref.shape
    n_total = dressed_ref.shape[1] // a_width
    n_pb, block_rows, _ = ladder_ref.shape
    c_block = block_rows // a_width
    size = Q_GROUP * a_width
    step = pl.program_id(0)

    @pl.when(step == 0)
    def _():
        n_occ = b_oc_ref.shape[1]
        row = lax.broadcasted_iota(jnp.int32, (size, a_width), 0)
        column = lax.broadcasted_iota(jnp.int32, (size, a_width), 1)
        tall = jnp.where(row % a_width == column, 1.0, 0.0).astype(jnp.bfloat16)
        row = lax.broadcasted_iota(jnp.int32, (n_occ, Q_GROUP * n_occ), 0)
        column = lax.broadcasted_iota(jnp.int32, (n_occ, Q_GROUP * n_occ), 1)
        wide = jnp.where(column % n_occ == row, 1.0, 0.0).astype(jnp.bfloat16)
        rows = jnp.dot(tall, t1_ref[...], preferred_element_type=jnp.float32).astype(jnp.bfloat16)
        repeated = jnp.dot(rows, wide, preferred_element_type=jnp.float32)
        row = lax.broadcasted_iota(jnp.int32, repeated.shape, 0)
        column = lax.broadcasted_iota(jnp.int32, repeated.shape, 1)
        same = row // a_width == column // n_occ
        singles_ref[...] = jnp.where(same, repeated, 0.0).astype(jnp.bfloat16)

    for group in range(n_q // Q_GROUP):
        rows = slice(group * Q_GROUP, (group + 1) * Q_GROUP)
        occupied = b_oc_ref[rows].reshape(-1, c_width)
        correction = jnp.dot(singles_ref[...], occupied, preferred_element_type=jnp.float32)
        block = b_ac_ref[rows].reshape(size, c_width).astype(jnp.float32)
        dressed = (block - correction).astype(jnp.bfloat16).astype(jnp.float32)
        at = pl.ds(pl.multiple_of((step * (n_q // Q_GROUP) + group) * size, size), size)
        for half in range(c_width // LANES):
            dressed_ref[half, at, :] = dressed[:, half * LANES : (half + 1) * LANES]

    @pl.when(step == pl.num_programs(0) - 1)
    def _():
        factors = f_ref[...]
        by_distance = (
            own_ref,
            up_ref.at[0],
            up2_ref,
            up_ref.at[1],
            across_ref,
            down_ref.at[1],
            down2_ref,
            down_ref.at[0],
        )
        here, way = place_ref[0] % n_pb, 1 - 2 * (place_ref[0] // n_pb)
        copies = []
        for a in range(a_width):
            for half in range(c_width // LANES):
                slab = dressed_ref.at[half][pl.ds(a, n_total, stride=a_width), :]
                part = lax.dot_general(
                    slab.astype(jnp.bfloat16),
                    factors,
                    (((0,), (0,)), ((), ())),
                    preferred_element_type=jnp.float32,
                ).astype(ladder_ref.dtype)
                for c_at in range(0, LANES, c_block):
                    ladder_ref[(half * LANES + c_at) // c_block, a * c_block : (a + 1) * c_block, :] = (
                        part[c_at : c_at + c_block]
                    )
            if (a + 1) % A_CHUNK == 0:
                chunk = a // A_CHUNK
                rows = pl.ds(chunk * A_CHUNK * c_block, A_CHUNK * c_block)
                for distance, out_ref in enumerate(by_distance):
                    copy = pltpu.make_async_copy(
                        ladder_ref.at[lax.rem(here + way * distance + n_pb, n_pb), rows],
                        out_ref.at[rows],
                        sems.at[chunk, distance],
                    )
                    copy.start()
                    copies.append(copy)
        for copy in copies:
            copy.wait()


def contract(b_ac, b_oc, t1, f_bd, place, n_pb):
    n_q, a_width, c_width = b_ac.shape
    n_occ = b_oc.shape[1]
    bd_width = f_bd.shape[1]
    block = (a_width * c_width // n_pb, bd_width)
    pair = (2, *block)
    shapes = (block, pair, block, block, block, pair)
    q_step = n_q // Q_STEPS
    return pl.pallas_call(
        contract_kernel,
        grid=(Q_STEPS,),
        out_shape=[jax.ShapeDtypeStruct(shape, jnp.bfloat16) for shape in shapes],
        in_specs=[
            SMEM,
            pl.BlockSpec((q_step, a_width, c_width), lambda step: (step, 0, 0)),
            pl.BlockSpec((q_step, n_occ, c_width), lambda step: (step, 0, 0)),
            pl.BlockSpec((a_width, n_occ), lambda step: (0, 0)),
            pl.BlockSpec(f_bd.shape, lambda step: (0, 0)),
        ],
        out_specs=[pl.BlockSpec(memory_space=pl.ANY)] * len(shapes),
        scratch_shapes=[
            pltpu.VMEM((Q_GROUP * a_width, Q_GROUP * n_occ), jnp.bfloat16),
            pltpu.VMEM((c_width // LANES, n_q * a_width, LANES), jnp.float32),
            pltpu.VMEM((n_pb, *block), jnp.bfloat16),
            pltpu.SemaphoreType.DMA((a_width // A_CHUNK, n_pb)),
        ],
        cost_estimate=pl.CostEstimate(
            flops=2 * n_q * a_width * c_width * bd_width, bytes_accessed=7 << 20, transcendentals=0
        ),
    )(place, b_ac, b_oc, t1.T, f_bd)


def merge_kernel(up_ref, down_ref, up2_ref, down2_ref, up_out, down_out):
    for passing_ref, own_ref, out_ref in (
        (up_ref, up2_ref, up_out),
        (down_ref, down2_ref, down_out),
    ):
        total = own_ref[...].astype(jnp.float32) + passing_ref[1].astype(jnp.float32)
        out_ref[...] = total.astype(out_ref.dtype)


def merge(up, down, up2, down2):
    return pl.pallas_call(
        merge_kernel,
        out_shape=[jax.ShapeDtypeStruct(up2.shape, up2.dtype)] * 2,
        in_specs=[VMEM] * 4,
        out_specs=[VMEM] * 2,
        compiler_params=pltpu.CompilerParams(vmem_limit_bytes=8 << 20),
        cost_estimate=pl.CostEstimate(flops=2 * up2.size, bytes_accessed=2 << 20, transcendentals=0),
    )(up, down, up2, down2)


def combine_kernel(
    own_ref, across_ref, up_ref, down_ref, up2_ref, down2_ref, t2_ref, out_ref, ladder_ref, turned_ref, *factor_refs
):
    total = own_ref[...].astype(jnp.float32)
    total += across_ref[...].astype(jnp.float32)
    total += up_ref[0].astype(jnp.float32)
    total += down_ref[0].astype(jnp.float32)
    total += up2_ref[...].astype(jnp.float32)
    total += down2_ref[...].astype(jnp.float32)
    for b_high in range(BB // LANE_GROUPS):
        ladder_ref[b_high] = total[:, b_high * LANES : (b_high + 1) * LANES]
    n_rows = total.shape[0] // LANE_GROUPS
    group = lax.broadcasted_iota(jnp.int32, (n_rows, LANES), 1) // DB

    def pick(by_group):
        chosen = by_group[0]
        for lane_group in range(1, LANE_GROUPS):
            chosen = jnp.where(group == lane_group, by_group[lane_group], chosen)
        return chosen

    for b_high in range(BB // LANE_GROUPS):
        by_c = [
            ladder_ref.at[b_high][pl.ds(c_low, n_rows, stride=LANE_GROUPS), :]
            for c_low in range(LANE_GROUPS)
        ]
        skewed = []
        for turn in range(LANE_GROUPS):
            mixed = pick([by_c[(b_low + turn) % LANE_GROUPS] for b_low in range(LANE_GROUPS)])
            skewed.append(pltpu.roll(mixed, turn * DB, 1) if turn else mixed)
        for b_low in range(LANE_GROUPS):
            b = b_high * LANE_GROUPS + b_low
            by_b = pick([skewed[(c_low - b_low) % LANE_GROUPS] for c_low in range(LANE_GROUPS)])
            for a in range(n_rows // BB):
                at = (a * BB + b) * BB
                turned_ref[at : at + BB, :] = by_b[a * BB : (a + 1) * BB]
    for c_high in range(BB):
        tile = turned_ref[pl.ds(c_high, n_rows, stride=BB), :]
        high = tile.astype(jnp.bfloat16)
        low = (tile - high.astype(jnp.float32)).astype(jnp.bfloat16)
        for factor_ref, factor in zip(factor_refs, (high, low)):
            factor_ref[:, c_high * LANES : (c_high + 1) * LANES] = factor
    sums = [
        lax.dot_general(
            t2_ref[...],
            factor_ref[...],
            (((1,), (1,)), ((), ())),
            preferred_element_type=jnp.float32,
        )
        for factor_ref in factor_refs
    ]
    out_ref[...] = (sums[0] + sums[1]).astype(out_ref.dtype)


def combine(parts, t2):
    block_rows, bd_width = parts[0].shape
    pairs, cd_width = t2.shape
    ab_width = block_rows * bd_width // cd_width
    return pl.pallas_call(
        combine_kernel,
        out_shape=jax.ShapeDtypeStruct((pairs, ab_width), jnp.bfloat16),
        in_specs=[VMEM] * (len(parts) + 1),
        out_specs=VMEM,
        scratch_shapes=[
            pltpu.VMEM((BB // LANE_GROUPS, block_rows, LANES), jnp.float32),
            pltpu.VMEM((ab_width * BB, LANES), jnp.float32),
            pltpu.VMEM((ab_width, cd_width), jnp.bfloat16),
            pltpu.VMEM((ab_width, cd_width), jnp.bfloat16),
        ],
        compiler_params=pltpu.CompilerParams(vmem_limit_bytes=16 << 20),
        cost_estimate=pl.CostEstimate(
            flops=2 * pairs * ab_width * cd_width, bytes_accessed=3 << 20, transcendentals=0
        ),
    )(*parts, t2)


def along_pb(array, distance):
    n_pb = lax.axis_size("pb")
    pairs = []
    for col in range(lax.axis_size("col")):
        way = -distance if col % 2 else distance
        pairs += [(col * n_pb + y, col * n_pb + (y + way) % n_pb) for y in range(n_pb)]
    return lax.ppermute(array, ("col", "pb"), pairs)


def step(b_ac, b_oc, t1, f_bd, t2):
    n_aa = lax.axis_size("aa")
    n_pb = lax.axis_size("pb")
    n_out = lax.axis_size("col") * n_pb
    core = lax.rem(lax.axis_index("col"), 2)
    place = (core * n_pb + lax.axis_index("pb")).astype(jnp.int32).reshape(1)

    amplitudes = lax.all_to_all(
        jnp.broadcast_to(t2[None], (n_aa, *t2.shape)), "aa", 0, 0, tiled=True
    ).reshape(-1, t2.shape[1])

    own, up, up2, across, down2, down = contract(b_ac, b_oc, t1, f_bd, place, n_pb)
    up = along_pb(up, 1)
    down = along_pb(down, -1)
    across = along_pb(across, 4)
    up2, down2 = merge(up, down, up2, down2)
    up2 = along_pb(up2, 2)
    down2 = along_pb(down2, -2)
    *parts, amplitudes = lax.optimization_barrier(
        (own, across, up, down, up2, down2, amplitudes)
    )
    sums = combine(parts, amplitudes)
    shares = sums.reshape(n_out, -1, sums.shape[1])
    shares = lax.all_to_all(shares, ("col", "pb"), 0, 0, tiled=True)
    return jnp.sum(shares.astype(jnp.float32), axis=0)


def solution(mesh):
    placed = (
        P("pb", "aa", "col"),
        P("pb", None, "col"),
        P(None, "aa"),
        P("pb", None),
        P("aa", ("col", "pb")),
    )
    return jax.shard_map(
        step, mesh=mesh, in_specs=placed, out_specs=P(("col", "pb"), "aa"), check_vma=False
    )
```

```python
import jax
import jax.numpy as jnp
from jax import lax
from jax.experimental import pallas as pl
from jax.experimental.pallas import tpu as pltpu
from jax.sharding import PartitionSpec as P


BB = 8
DB = 32
LANES = 128
LANE_GROUPS = LANES // DB
Q_GROUP = 8
Q_STEPS = 4
A_CHUNK = 4
VMEM = pl.BlockSpec(memory_space=pltpu.VMEM)
SMEM = pl.BlockSpec(memory_space=pltpu.SMEM)


def contract_kernel(place_ref, b_ac_ref, b_oc_ref, t1_ref, f_ref, t2_ref, *refs):
    out_refs, (singles_ref, dressed_ref, ladder_ref, sems, t2_sems) = refs[:-5], refs[-5:]
    own_ref, up_ref, up2_ref, across_ref, down2_ref, down_ref, repeats_ref = out_refs
    n_q, a_width, c_width = b_ac_ref.shape
    n_total = dressed_ref.shape[1] // a_width
    n_pb, block_rows, _ = ladder_ref.shape
    c_block = block_rows // a_width
    size = Q_GROUP * a_width
    step = pl.program_id(0)

    @pl.when(step == 0)
    def _():
        n_occ = b_oc_ref.shape[1]
        row = lax.broadcasted_iota(jnp.int32, (size, a_width), 0)
        column = lax.broadcasted_iota(jnp.int32, (size, a_width), 1)
        tall = jnp.where(row % a_width == column, 1.0, 0.0).astype(jnp.bfloat16)
        row = lax.broadcasted_iota(jnp.int32, (n_occ, Q_GROUP * n_occ), 0)
        column = lax.broadcasted_iota(jnp.int32, (n_occ, Q_GROUP * n_occ), 1)
        wide = jnp.where(column % n_occ == row, 1.0, 0.0).astype(jnp.bfloat16)
        rows = jnp.dot(tall, t1_ref[...], preferred_element_type=jnp.float32).astype(jnp.bfloat16)
        repeated = jnp.dot(rows, wide, preferred_element_type=jnp.float32)
        row = lax.broadcasted_iota(jnp.int32, repeated.shape, 0)
        column = lax.broadcasted_iota(jnp.int32, repeated.shape, 1)
        same = row // a_width == column // n_occ
        singles_ref[...] = jnp.where(same, repeated, 0.0).astype(jnp.bfloat16)

    for group in range(n_q // Q_GROUP):
        rows = slice(group * Q_GROUP, (group + 1) * Q_GROUP)
        occupied = b_oc_ref[rows].reshape(-1, c_width)
        correction = jnp.dot(singles_ref[...], occupied, preferred_element_type=jnp.float32)
        block = b_ac_ref[rows].reshape(size, c_width).astype(jnp.float32)
        dressed = (block - correction).astype(jnp.bfloat16).astype(jnp.float32)
        at = pl.ds(pl.multiple_of((step * (n_q // Q_GROUP) + group) * size, size), size)
        for half in range(c_width // LANES):
            dressed_ref[half, at, :] = dressed[:, half * LANES : (half + 1) * LANES]

    @pl.when(step == pl.num_programs(0) - 1)
    def _():
        factors = f_ref[...]
        by_distance = (
            own_ref,
            up_ref.at[0],
            up2_ref,
            up_ref.at[1],
            across_ref,
            down_ref.at[1],
            down2_ref,
            down_ref.at[0],
        )
        repeats = [
            pltpu.make_async_copy(t2_ref, repeats_ref.at[at], t2_sems.at[at])
            for at in range(repeats_ref.shape[0])
        ]
        for copy in repeats:
            copy.start()
        here, way = place_ref[0] % n_pb, 1 - 2 * (place_ref[0] // n_pb)
        copies = []
        for a in range(a_width):
            for half in range(c_width // LANES):
                slab = dressed_ref.at[half][pl.ds(a, n_total, stride=a_width), :]
                part = lax.dot_general(
                    slab.astype(jnp.bfloat16),
                    factors,
                    (((0,), (0,)), ((), ())),
                    preferred_element_type=jnp.float32,
                ).astype(ladder_ref.dtype)
                for c_at in range(0, LANES, c_block):
                    ladder_ref[(half * LANES + c_at) // c_block, a * c_block : (a + 1) * c_block, :] = (
                        part[c_at : c_at + c_block]
                    )
            if (a + 1) % A_CHUNK == 0:
                chunk = a // A_CHUNK
                rows = pl.ds(chunk * A_CHUNK * c_block, A_CHUNK * c_block)
                for distance, out_ref in enumerate(by_distance):
                    copy = pltpu.make_async_copy(
                        ladder_ref.at[lax.rem(here + way * distance + n_pb, n_pb), rows],
                        out_ref.at[rows],
                        sems.at[chunk, distance],
                    )
                    copy.start()
                    copies.append(copy)
        for copy in copies + repeats:
            copy.wait()


def contract(b_ac, b_oc, t1, f_bd, t2, place, n_pb, n_aa):
    n_q, a_width, c_width = b_ac.shape
    n_occ = b_oc.shape[1]
    bd_width = f_bd.shape[1]
    block = (a_width * c_width // n_pb, bd_width)
    pair = (2, *block)
    shapes = (block, pair, block, block, block, pair, (n_aa, *t2.shape))
    q_step = n_q // Q_STEPS
    return pl.pallas_call(
        contract_kernel,
        grid=(Q_STEPS,),
        out_shape=[jax.ShapeDtypeStruct(shape, jnp.bfloat16) for shape in shapes],
        in_specs=[
            SMEM,
            pl.BlockSpec((q_step, a_width, c_width), lambda step: (step, 0, 0)),
            pl.BlockSpec((q_step, n_occ, c_width), lambda step: (step, 0, 0)),
            pl.BlockSpec((a_width, n_occ), lambda step: (0, 0)),
            pl.BlockSpec(f_bd.shape, lambda step: (0, 0)),
            pl.BlockSpec(t2.shape, lambda step: (0, 0)),
        ],
        out_specs=[pl.BlockSpec(memory_space=pl.ANY)] * len(shapes),
        scratch_shapes=[
            pltpu.VMEM((Q_GROUP * a_width, Q_GROUP * n_occ), jnp.bfloat16),
            pltpu.VMEM((c_width // LANES, n_q * a_width, LANES), jnp.float32),
            pltpu.VMEM((n_pb, *block), jnp.bfloat16),
            pltpu.SemaphoreType.DMA((a_width // A_CHUNK, n_pb)),
            pltpu.SemaphoreType.DMA((n_aa,)),
        ],
        cost_estimate=pl.CostEstimate(
            flops=2 * n_q * a_width * c_width * bd_width, bytes_accessed=7 << 20, transcendentals=0
        ),
    )(place, b_ac, b_oc, t1.T, f_bd, t2)


def merge_kernel(up_ref, down_ref, up2_ref, down2_ref, up_out, down_out):
    for passing_ref, own_ref, out_ref in (
        (up_ref, up2_ref, up_out),
        (down_ref, down2_ref, down_out),
    ):
        total = own_ref[...].astype(jnp.float32) + passing_ref[1].astype(jnp.float32)
        out_ref[...] = total.astype(out_ref.dtype)


def merge(up, down, up2, down2):
    return pl.pallas_call(
        merge_kernel,
        out_shape=[jax.ShapeDtypeStruct(up2.shape, up2.dtype)] * 2,
        in_specs=[VMEM] * 4,
        out_specs=[VMEM] * 2,
        compiler_params=pltpu.CompilerParams(vmem_limit_bytes=8 << 20),
        cost_estimate=pl.CostEstimate(flops=2 * up2.size, bytes_accessed=2 << 20, transcendentals=0),
    )(up, down, up2, down2)


def combine_kernel(
    own_ref, across_ref, up_ref, down_ref, up2_ref, down2_ref, t2_ref, out_ref, ladder_ref, turned_ref, *factor_refs
):
    total = own_ref[...].astype(jnp.float32)
    total += across_ref[...].astype(jnp.float32)
    total += up_ref[0].astype(jnp.float32)
    total += down_ref[0].astype(jnp.float32)
    total += up2_ref[...].astype(jnp.float32)
    total += down2_ref[...].astype(jnp.float32)
    for b_high in range(BB // LANE_GROUPS):
        ladder_ref[b_high] = total[:, b_high * LANES : (b_high + 1) * LANES]
    n_rows = total.shape[0] // LANE_GROUPS
    group = lax.broadcasted_iota(jnp.int32, (n_rows, LANES), 1) // DB

    def pick(by_group):
        chosen = by_group[0]
        for lane_group in range(1, LANE_GROUPS):
            chosen = jnp.where(group == lane_group, by_group[lane_group], chosen)
        return chosen

    for b_high in range(BB // LANE_GROUPS):
        by_c = [
            ladder_ref.at[b_high][pl.ds(c_low, n_rows, stride=LANE_GROUPS), :]
            for c_low in range(LANE_GROUPS)
        ]
        skewed = []
        for turn in range(LANE_GROUPS):
            mixed = pick([by_c[(b_low + turn) % LANE_GROUPS] for b_low in range(LANE_GROUPS)])
            skewed.append(pltpu.roll(mixed, turn * DB, 1) if turn else mixed)
        for b_low in range(LANE_GROUPS):
            b = b_high * LANE_GROUPS + b_low
            by_b = pick([skewed[(c_low - b_low) % LANE_GROUPS] for c_low in range(LANE_GROUPS)])
            for a in range(n_rows // BB):
                at = (a * BB + b) * BB
                turned_ref[at : at + BB, :] = by_b[a * BB : (a + 1) * BB]
    for c_high in range(BB):
        tile = turned_ref[pl.ds(c_high, n_rows, stride=BB), :]
        high = tile.astype(jnp.bfloat16)
        low = (tile - high.astype(jnp.float32)).astype(jnp.bfloat16)
        for factor_ref, factor in zip(factor_refs, (high, low)):
            factor_ref[:, c_high * LANES : (c_high + 1) * LANES] = factor
    sums = [
        lax.dot_general(
            t2_ref[...],
            factor_ref[...],
            (((1,), (1,)), ((), ())),
            preferred_element_type=jnp.float32,
        )
        for factor_ref in factor_refs
    ]
    out_ref[...] = (sums[0] + sums[1]).astype(out_ref.dtype)


def combine(parts, t2):
    block_rows, bd_width = parts[0].shape
    pairs, cd_width = t2.shape
    ab_width = block_rows * bd_width // cd_width
    return pl.pallas_call(
        combine_kernel,
        out_shape=jax.ShapeDtypeStruct((pairs, ab_width), jnp.bfloat16),
        in_specs=[VMEM] * (len(parts) + 1),
        out_specs=VMEM,
        scratch_shapes=[
            pltpu.VMEM((BB // LANE_GROUPS, block_rows, LANES), jnp.float32),
            pltpu.VMEM((ab_width * BB, LANES), jnp.float32),
            pltpu.VMEM((ab_width, cd_width), jnp.bfloat16),
            pltpu.VMEM((ab_width, cd_width), jnp.bfloat16),
        ],
        compiler_params=pltpu.CompilerParams(vmem_limit_bytes=16 << 20),
        cost_estimate=pl.CostEstimate(
            flops=2 * pairs * ab_width * cd_width, bytes_accessed=3 << 20, transcendentals=0
        ),
    )(*parts, t2)


def along_pb(array, distance):
    n_pb = lax.axis_size("pb")
    pairs = []
    for col in range(lax.axis_size("col")):
        way = -distance if col % 2 else distance
        pairs += [(col * n_pb + y, col * n_pb + (y + way) % n_pb) for y in range(n_pb)]
    return lax.ppermute(array, ("col", "pb"), pairs)


def step(b_ac, b_oc, t1, f_bd, t2):
    n_aa = lax.axis_size("aa")
    n_pb = lax.axis_size("pb")
    n_out = lax.axis_size("col") * n_pb
    core = lax.rem(lax.axis_index("col"), 2)
    place = (core * n_pb + lax.axis_index("pb")).astype(jnp.int32).reshape(1)

    own, up, up2, across, down2, down, repeats = contract(
        b_ac, b_oc, t1, f_bd, t2, place, n_pb, n_aa
    )
    amplitudes = lax.all_to_all(repeats, "aa", 0, 0, tiled=True).reshape(-1, t2.shape[1])
    up = along_pb(up, 1)
    down = along_pb(down, -1)
    across = along_pb(across, 4)
    up2, down2 = merge(up, down, up2, down2)
    up2 = along_pb(up2, 2)
    down2 = along_pb(down2, -2)
    *parts, amplitudes = lax.optimization_barrier(
        (own, across, up, down, up2, down2, amplitudes)
    )
    sums = combine(parts, amplitudes)
    shares = sums.reshape(n_out, -1, sums.shape[1])
    shares = lax.all_to_all(shares, ("col", "pb"), 0, 0, tiled=True)
    return jnp.sum(shares.astype(jnp.float32), axis=0)


def solution(mesh):
    placed = (
        P("pb", "aa", "col"),
        P("pb", None, "col"),
        P(None, "aa"),
        P("pb", None),
        P("aa", ("col", "pb")),
    )
    return jax.shard_map(
        step, mesh=mesh, in_specs=placed, out_specs=P(("col", "pb"), "aa"), check_vma=False
    )
```
